32 devices in a mesh: groups: 2 (over x), ctx: 16 (over z, y, core).
Axes of the slice: x: 2, y: 2, z: 4, core: 2. Of those that a mesh axis runs over, the one named last changes fastest.
Arguments:
- tokens: bfloat16 [12288, 1536], P(('groups', 'ctx')), parts along dimension 0, may hold values from -6 to 6
- dilated_weight: bfloat16 [1536, 3, 384], P('ctx'), may hold values from -0.09375 to 0.09375
- pointwise_weight: bfloat16 [384, 1536], P('ctx'), may hold values from -0.3125 to 0.3125
- query_key_value_weight: bfloat16 [1536, 1280], P('ctx'), may hold values from -1 to 3
- slopes: float32 [4], replicated, may hold values from 0.002 to 0.06
- chain_labels: int32 [12288], P('groups'), parts along dimension 0, may hold values from 0 to 3, never falling along the last dimension, each value on 1 to 3072 neighbouring positions
- attention_cotangent: bfloat16 [12288, 768], P(('groups', 'ctx')), parts along dimension 0, may hold values from -6 to 6
Outputs:
- attended: bfloat16 [12288, 768], P(('groups', 'ctx')), parts along dimension 0
- dilated_kernel_grad: float32 [3072, 3, 384], P(('groups', 'ctx')), parts along dimension 0
- pointwise_kernel_grad: float32 [768, 1536], P(('groups', 'ctx')), parts along dimension 0
The draws below stay inside these ranges and needn't reach their ends.
There are 2 independent parts, one for each index of `groups`. The reference program is written for one: setup_inputs(seed, part) draws one part's arguments, and reference() takes and returns one part's arrays. A program takes and returns all parts, laid end to end along the dimension named above; an argument that names none is the same for every part. Nothing has to cross between parts.
Inputs may be any that keep to these rules, and one draw needn't show every extreme that they name: chain_labels never falls along positions; each chain covers 1 to 3072 positions, one exactly 3072.
All inputs are finite; a program needn't handle non-finite values.
Results may differ from the reference program's by a relative error of at most 0.018.
The reference program's roundings to bfloat16 on the way count: a program that leaves them out, or rounds other values in their place, can miss the bound.
Values may be sent and summed in bfloat16 or wider, within the bound.
No kernel may reach another device: no remote copies, remote signals or barrier semaphores. Data moves between devices by JAX's collectives and lax.ppermute only.
A program may use at most 128 MiB of HBM per device.

```python
import math
import jax
import jax.numpy as jnp
import numpy as np
from jax import lax

MODEL_CHANNELS = 1536
NARROW_CHANNELS = 384
HEADS = 4
KEY = 64
VAL = 192
DILATION_STEP = 16
ROWS = 384
TOKENS = 6144
QKW = 1280
CHAINS = 4


def draw_query_key_value_weight(key, part):
    normal_part = jnp.clip(jax.random.normal(key, (MODEL_CHANNELS, QKW), jnp.float32), -6.0, 6.0) / math.sqrt(MODEL_CHANNELS)
    return normal_part.astype(jnp.bfloat16)


def strengthened(result, own_key, source, target, shards_of, factor):
    owner, partner = [(jnp.arange(result.shape[position]) // (result.shape[position] // shards_of)).reshape([-1 if axis == position else 1 for axis in range(result.ndim)]) for position in (source, target)]
    chosen = jax.random.permutation(own_key, shards_of)[partner]
    strong = (owner == chosen) | (owner == (partner + shards_of // 2) % shards_of)
    return jnp.where(strong, factor * result, result)


def shard_levels(rng, dims, pieces, smallest, top_value):
    gain = 1.0
    for position, parts in pieces:
        draws = jax.random.uniform(jax.random.fold_in(jax.random.fold_in(rng, 6), position), (parts,), jnp.float32, smallest / len(pieces), top_value / len(pieces))
        gain = gain * jnp.repeat(jnp.exp(draws), dims[position] // parts).reshape((-1,) + (1,) * (len(dims) - 1 - position))
    return gain


def split_up(count, total, limit, skew):
    loads = [(1 << 20) // math.isqrt(standing ** skew) + 1 for standing in range(2, count + 1)]
    rest, given = total - limit - (count - 1), [1] * (count - 1)
    while rest > 0:
        candidates = [i for i in range(count - 1) if given[i] < limit]
        mass, left = sum([loads[i] for i in candidates]), rest
        for i in candidates:
            more = min(limit - given[i], max(1, left * loads[i] // mass), rest)
            given[i] = given[i] + more
            rest = rest - more
    return np.array([limit] + given)


def ragged_sizes(own_key, number_of, total, bound, skew):
    if number_of == 2:
        one = jax.random.randint(own_key, (), max(1, total - bound), min(bound, total - 1) + 1)
        return jnp.stack([one, total - one])
    sizes = jnp.asarray(split_up(number_of, total, bound, skew), jnp.int32)
    pairs = (number_of - 1) // 2
    giver, taker = sizes[1:1 + 2 * pairs:2], sizes[2:2 + 2 * pairs:2]
    slack = jnp.minimum(giver - 1, bound - taker)
    shifted = jax.random.randint(jax.random.fold_in(own_key, 1), (pairs,), 0, 1 << 20) % (slack + 1)
    sizes = sizes.at[1:1 + 2 * pairs:2].set(giver - shifted).at[2:2 + 2 * pairs:2].set(taker + shifted)
    return sizes[jax.random.permutation(jax.random.fold_in(own_key, 2), number_of)]


def noise(stream_key, shape, scale, bound, shards=(), kind=jnp.bfloat16):
    drawn = scale * jax.random.normal(stream_key, shape, jnp.float32)
    if shards:
        drawn = drawn * shard_levels(stream_key, shape, shards, -0.22, 0.18)
    return jnp.clip(drawn, -bound, bound).astype(kind)


def bell_draw_with(key, shape, deviation, bound, split, heavy, held_as=jnp.bfloat16):
    drawn = deviation * jax.random.normal(key, shape, jnp.float32)
    if split:
        drawn = drawn * shard_levels(key, shape, split, -0.22, 0.18)
    return jnp.clip(strengthened(drawn, jax.random.fold_in(key, 3), *heavy), -bound, bound).astype(held_as)


def setup_inputs(seed: int = 0, part: int = 0) -> dict:
    arg_keys = jax.random.split(jax.random.key(seed), 8)
    part_keys = jax.random.split(jax.random.fold_in(arg_keys[7], part), 8)
    return {
        "tokens": bell_draw_with(part_keys[0], (TOKENS, MODEL_CHANNELS), 1.0, 6.0, ((0, 16),), (0, 1, 16, 2.0)),
        "dilated_weight": noise(arg_keys[1], (MODEL_CHANNELS, 3, NARROW_CHANNELS), (3 * MODEL_CHANNELS) ** -0.5, 0.09375, ((0, 16),)),
        "pointwise_weight": noise(arg_keys[2], (NARROW_CHANNELS, MODEL_CHANNELS), NARROW_CHANNELS ** -0.5, 0.3125, ((0, 16),)),
        "query_key_value_weight": draw_query_key_value_weight(jax.random.fold_in(arg_keys[7], 71), part),
        "slopes": jnp.clip(jnp.exp(jax.random.uniform(arg_keys[4], (HEADS,), jnp.float32, math.log(0.002), math.log(0.06))), 0.002, 0.06),
        "chain_labels": jnp.searchsorted(jnp.cumsum(ragged_sizes(part_keys[5], CHAINS, TOKENS, 8 * ROWS, 2)), jnp.arange(TOKENS), side="right").astype(jnp.int32),
        "attention_cotangent": noise(part_keys[6], (TOKENS, HEADS * VAL), 1.0, 6.0, ((0, 16),)),
    }


NEG_FILL = -1e+30

def head_scores(q_head, k_head, slope, qpos, kpos, qchain, kchain, total_sum):
    scores = jnp.dot(q_head, k_head.T, preferred_element_type=jnp.float32) * (1.0 / math.sqrt(KEY))
    spread = jnp.abs(qpos[:, None] - kpos[None, :]).astype(jnp.float32)
    scores = scores - slope * spread
    inside_q = (qpos >= 0) & (qpos < total_sum)
    inside_k = (kpos >= 0) & (kpos < total_sum)
    allowed = inside_q[:, None] & inside_k[None, :] & (qchain[:, None] == kchain[None, :])
    return jnp.where(allowed, scores, NEG_FILL)

def attend(queries, keyvals, slopes, qpos, kpos, qchain, kchain, total_sum):
    key_cols = HEADS * KEY
    outputs = []
    totals = []
    for head in range(HEADS):
        q_head = queries[:, head * KEY:(head + 1) * KEY]
        k_head = keyvals[:, head * KEY:(head + 1) * KEY]
        v_head = keyvals[:, key_cols + head * VAL:key_cols + (head + 1) * VAL]
        scores = head_scores(q_head, k_head, slopes[head], qpos, kpos, qchain, kchain, total_sum)
        top = lax.optimization_barrier(jnp.max(scores, axis=1, keepdims=True))
        expo = jnp.exp(scores - top)
        denom = lax.optimization_barrier(jnp.sum(expo, axis=1, keepdims=True))
        weights = (expo / denom).astype(jnp.bfloat16)
        outputs.append(jnp.dot(weights, v_head, preferred_element_type=jnp.float32))
        totals.append(top[:, 0] + jnp.log(denom[:, 0]))
    return (jnp.concatenate(outputs, axis=1), jnp.stack(totals, axis=1))

def attend_grads(queries, keyvals, d_out, lse, delta, slopes, qpos, kpos, qchain, kchain, total_sum):
    key_cols = HEADS * KEY
    scale = 1.0 / math.sqrt(KEY)
    d_query = []
    d_key = []
    d_value = []
    for head in range(HEADS):
        q_head = queries[:, head * KEY:(head + 1) * KEY]
        k_head = keyvals[:, head * KEY:(head + 1) * KEY]
        v_head = keyvals[:, key_cols + head * VAL:key_cols + (head + 1) * VAL]
        d_head = d_out[:, head * VAL:(head + 1) * VAL]
        scores = head_scores(q_head, k_head, slopes[head], qpos, kpos, qchain, kchain, total_sum)
        back = jnp.exp(scores - lse[:, head:head + 1])
        d_prob = jnp.dot(d_head, v_head.T, preferred_element_type=jnp.float32)
        d_score = (back * (d_prob - delta[:, head:head + 1]) * scale).astype(jnp.bfloat16)
        back_w = back.astype(jnp.bfloat16)
        d_query.append(jnp.dot(d_score, k_head, preferred_element_type=jnp.float32))
        d_key.append(jnp.dot(d_score.T, q_head, preferred_element_type=jnp.float32))
        d_value.append(jnp.dot(back_w.T, d_head, preferred_element_type=jnp.float32))
    return (jnp.concatenate(d_query, axis=1), jnp.concatenate(d_key + d_value, axis=1))

def reference(tokens, dilated_weight, pointwise_weight, query_key_value_weight, slopes, chain_labels, attention_cotangent):
    total_sum = tokens.shape[0]
    nblocks = total_sum // ROWS
    padded_input = jnp.pad(tokens, ((DILATION_STEP, DILATION_STEP), (0, 0)))
    tap_outputs = [padded_input[tap_index * DILATION_STEP:tap_index * DILATION_STEP + total_sum] for tap_index in range(3)]
    preactivation = jnp.dot(tap_outputs[0], dilated_weight[:, 0, :], preferred_element_type=jnp.float32)
    preactivation = preactivation + jnp.dot(tap_outputs[1], dilated_weight[:, 1, :], preferred_element_type=jnp.float32)
    preactivation = preactivation + jnp.dot(tap_outputs[2], dilated_weight[:, 2, :], preferred_element_type=jnp.float32)
    hidden = jax.nn.gelu(preactivation).astype(jnp.bfloat16)
    mixed = tokens.astype(jnp.float32) + jnp.dot(hidden, pointwise_weight, preferred_element_type=jnp.float32)
    inv = lax.rsqrt(lax.optimization_barrier(jnp.mean(mixed * mixed, axis=1, keepdims=True)) + 1e-06)
    normed = (mixed * inv).astype(jnp.bfloat16)
    qkv = jnp.dot(normed, query_key_value_weight, preferred_element_type=jnp.float32).astype(jnp.bfloat16)
    key_cols = HEADS * KEY
    queries = qkv[:, :key_cols]
    keyvals = qkv[:, key_cols:]
    kv_pad = jnp.pad(keyvals, ((ROWS, ROWS), (0, 0)))
    chain_pad = jnp.pad(chain_labels, (ROWS, ROWS), constant_values=-1)

    def block_view(block):
        start = block.astype(jnp.int32) * ROWS
        qpos = start + jnp.arange(ROWS, dtype=jnp.int32)
        kpos = start - ROWS + jnp.arange(3 * ROWS, dtype=jnp.int32)
        qchain = lax.dynamic_slice_in_dim(chain_labels, start, ROWS)
        kchain = lax.dynamic_slice_in_dim(chain_pad, start, 3 * ROWS)
        q_block = lax.dynamic_slice_in_dim(queries, start, ROWS, 0)
        kv_block = lax.dynamic_slice_in_dim(kv_pad, start, 3 * ROWS, 0)
        return (start, qpos, kpos, qchain, kchain, q_block, kv_block)

    def forward_block(block):
        start, qpos, kpos, qchain, kchain, q_block, kv_block = block_view(block)
        return attend(q_block, kv_block, slopes, qpos, kpos, qchain, kchain, total_sum)
    out_blocks, lse_blocks = lax.map(forward_block, jnp.arange(nblocks, dtype=jnp.int32))
    out = out_blocks.reshape(total_sum, HEADS * VAL)
    lse = lse_blocks.reshape(total_sum, HEADS)
    attended = out.astype(jnp.bfloat16)
    delta = lax.optimization_barrier(jnp.sum((attention_cotangent.astype(jnp.float32) * out).reshape(total_sum, HEADS, VAL), axis=2))

    def backward_block(block, carry):
        d_query_all, dkv_pad = carry
        start, qpos, kpos, qchain, kchain, q_block, kv_block = block_view(jnp.asarray(block, jnp.int32))
        d_block = lax.dynamic_slice_in_dim(attention_cotangent, start, ROWS, 0)
        lse_block = lax.dynamic_slice_in_dim(lse, start, ROWS, 0)
        delta_block = lax.dynamic_slice_in_dim(delta, start, ROWS, 0)
        d_query, d_kv = attend_grads(q_block, kv_block, d_block, lse_block, delta_block, slopes, qpos, kpos, qchain, kchain, total_sum)
        d_query_all = lax.dynamic_update_slice_in_dim(d_query_all, d_query, start, 0)
        previous = lax.dynamic_slice_in_dim(dkv_pad, start, 3 * ROWS, 0)
        dkv_pad = lax.dynamic_update_slice_in_dim(dkv_pad, previous + d_kv, start, 0)
        return (d_query_all, dkv_pad)
    start_carry = (jnp.zeros((total_sum, key_cols), jnp.float32), jnp.zeros((total_sum + 2 * ROWS, keyvals.shape[1]), jnp.float32))
    d_query_all, dkv_pad = lax.fori_loop(0, nblocks, backward_block, start_carry)
    d_qkv = jnp.concatenate([d_query_all, dkv_pad[ROWS:ROWS + total_sum]], axis=1).astype(jnp.bfloat16)
    d_normed = jnp.dot(d_qkv, query_key_value_weight.T, preferred_element_type=jnp.float32)
    d_mixed = (inv * d_normed - mixed * inv ** 3 * lax.optimization_barrier(jnp.mean(d_normed * mixed, axis=1, keepdims=True))).astype(jnp.bfloat16)
    pointwise_kernel_grad = jnp.dot(hidden.T, d_mixed, preferred_element_type=jnp.float32)
    d_hidden = jnp.dot(d_mixed, pointwise_weight.T, preferred_element_type=jnp.float32)
    slope_fn = jax.vjp(jax.nn.gelu, preactivation)[1]
    preactivation_grad = slope_fn(d_hidden)[0].astype(jnp.bfloat16)
    dilated_kernel_grad = jnp.stack([jnp.dot(tap_outputs[tap_index].T, preactivation_grad, preferred_element_type=jnp.float32) for tap_index in range(3)], axis=1)
    return (attended, dilated_kernel_grad, pointwise_kernel_grad)
```

```python
import functools
import math

import jax
import jax.numpy as jnp
from jax import lax
from jax.experimental import pallas as pl
from jax.experimental.pallas import tpu as pltpu
from jax.sharding import PartitionSpec as P

HEADS = 4
KEY = 64
VAL = 192
DILATION_STEP = 16
KEY_COLS = HEADS * KEY
NEG_FILL = -1e30
SCALE = 1.0 / math.sqrt(KEY)
GELU_C = math.sqrt(2.0 / math.pi)
PIECES = 16

F32 = jnp.float32
BF16 = jnp.bfloat16
VMEM = pl.BlockSpec(memory_space=pltpu.VMEM)
SMEM = pl.BlockSpec(memory_space=pltpu.SMEM)
ANY = pl.BlockSpec(memory_space=pl.ANY)


def dot(a, b):
    return jnp.dot(a, b, preferred_element_type=F32)


def dot_t(a, b):
    return lax.dot_general(a, b, (((1,), (1,)), ((), ())), preferred_element_type=F32)


def params(mib):
    return pltpu.CompilerParams(vmem_limit_bytes=mib << 20)


def conv_kernel(index, tokens, *refs):
    pieces, (pre, hidden, weight, sems) = refs[:PIECES], refs[PIECES:]
    rows = pieces[0].shape[0]
    copies = []
    for i, piece in enumerate(pieces):
        start = pl.multiple_of(index[i] * rows, rows)
        copies.append(pltpu.make_async_copy(piece, weight.at[pl.ds(start, rows)], sems.at[i]))
    for copy in copies:
        copy.start()
    for copy in copies:
        copy.wait()
    count, narrow = pre.shape
    total = None
    for tap in range(3):
        part = dot(
            tokens[tap * DILATION_STEP : tap * DILATION_STEP + count, :],
            weight[:, tap * narrow : (tap + 1) * narrow],
        )
        total = part if total is None else total + part
    pre[...] = total
    inner = jnp.tanh(GELU_C * (total + 0.044715 * (total * total * total)))
    hidden[...] = (total * (0.5 * (1.0 + inner))).astype(BF16)


def project_kernel(index, tokens, hidden, *refs):
    pieces = refs[:PIECES]
    mixed, inv, qkv, projection, point, blocks, wide, sems = refs[PIECES:]
    rows = pieces[0].shape[0]
    columns = projection.shape[1]
    count = mixed.shape[0]
    copies = []
    for i, piece in enumerate(pieces):
        start = pl.multiple_of(index[i] * rows, rows)
        copies.append(
            pltpu.make_async_copy(
                piece.at[:, columns:], blocks.at[i], sems.at[0, i]
            )
        )
        copies.append(
            pltpu.make_async_copy(
                piece.at[:, :columns], projection.at[pl.ds(start, rows)], sems.at[1, i]
            )
        )
    for copy in copies:
        copy.start()
    for copy in copies[::2]:
        copy.wait()
    slim = rows // 4
    width = blocks.shape[2]
    for i in range(PIECES):
        block = blocks[i].astype(F32)
        start = pl.multiple_of(index[i] * slim, 8)
        for j in range(4):
            wide[pl.ds(start, slim), j * width : (j + 1) * width] = block[
                j * slim : (j + 1) * slim
            ]
    point[...] = wide[...].astype(BF16)
    mix = tokens[DILATION_STEP : DILATION_STEP + count, :].astype(F32) + dot(
        hidden[...], point[...]
    )
    mixed[...] = mix
    scale = lax.rsqrt(jnp.mean(mix * mix, axis=1, keepdims=True) + 1e-06)
    inv[...] = scale
    normed = (mix * scale).astype(BF16)
    for copy in copies[1::2]:
        copy.wait()
    qkv[...] = dot(normed, projection[...]).astype(BF16)


def distance(shape, shift):
    a = lax.broadcasted_iota(jnp.int32, shape, 0)
    b = lax.broadcasted_iota(jnp.int32, shape, 1)
    return jnp.abs(a - b + shift).astype(F32)


def attend_kernel(
    slopes, query, kv_prev, kv, kv_next, d_out, q_chain, k_prev, k_own, k_next, *refs
):
    attended, d_query, stats = refs
    count = query.shape[0]
    near = (kv_prev, kv, kv_next)
    away = [distance((count, count), shift) for shift in (count, 0, -count)]
    same = [q_chain[...] == chain[...] for chain in (k_prev, k_own, k_next)]
    tops, deltas = [], []
    for head in range(HEADS):
        kcols = slice(head * KEY, (head + 1) * KEY)
        vcols = slice(KEY_COLS + head * VAL, KEY_COLS + (head + 1) * VAL)
        ocols = slice(head * VAL, (head + 1) * VAL)
        q = query[:, kcols]
        slope = slopes[head]
        scores = []
        for i in range(3):
            score = dot_t(q, near[i][:, kcols]) * SCALE - slope * away[i]
            scores.append(jnp.where(same[i], score, NEG_FILL))
        top = functools.reduce(
            jnp.maximum, [jnp.max(s, axis=1, keepdims=True) for s in scores]
        )
        expo = [jnp.exp(s - top) for s in scores]
        denom = sum(jnp.sum(e, axis=1, keepdims=True) for e in expo)
        share = 1.0 / denom
        prob = [e * share for e in expo]
        out = sum(dot(p.astype(BF16), near[i][:, vcols]) for i, p in enumerate(prob))
        attended[:, ocols] = out.astype(BF16)
        d_head = d_out[:, ocols]
        delta = jnp.sum(d_head.astype(F32) * out, axis=1, keepdims=True)
        d_q = None
        for i in range(3):
            d_prob = dot_t(d_head, near[i][:, vcols])
            d_score = (prob[i] * (d_prob - delta) * SCALE).astype(BF16)
            part = dot(d_score, near[i][:, kcols])
            d_q = part if d_q is None else d_q + part
        d_query[:, kcols] = d_q.astype(BF16)
        tops.append(top + jnp.log(denom))
        deltas.append(delta)
    pad = jnp.zeros((count, 128 - 2 * HEADS), F32)
    packed = jnp.concatenate(tops + deltas + [pad], axis=1)
    stats[...] = packed.T[: 2 * HEADS]


def key_grad_kernel(slopes, kv, k_chain, *refs):
    groups, (d_kv,) = [refs[5 * i : 5 * i + 5] for i in range(3)], refs[15:]
    count = kv.shape[0]
    away = [distance((count, count), shift) for shift in (count, 0, -count)]
    same = [k_chain[...] == group[4][...] for group in groups]
    for head in range(HEADS):
        kcols = slice(head * KEY, (head + 1) * KEY)
        vcols = slice(KEY_COLS + head * VAL, KEY_COLS + (head + 1) * VAL)
        ocols = slice(head * VAL, (head + 1) * VAL)
        k, v, slope = kv[:, kcols], kv[:, vcols], slopes[head]
        d_k = d_v = None
        for i, (query, d_out, stats, _, _) in enumerate(groups):
            q, d_head = query[:, kcols], d_out[:, ocols]
            score = dot_t(k, q) * SCALE - slope * away[i]
            score = jnp.where(same[i], score, NEG_FILL)
            back = jnp.exp(score - stats[head : head + 1, :])
            back = jnp.where(same[i], back, 0.0)
            d_prob = dot_t(v, d_head)
            d_score = back * (d_prob - stats[HEADS + head : HEADS + head + 1, :]) * SCALE
            part_k, part_v = dot(d_score.astype(BF16), q), dot(back.astype(BF16), d_head)
            d_k = part_k if d_k is None else d_k + part_k
            d_v = part_v if d_v is None else d_v + part_v
        d_kv[:, kcols] = d_k.astype(BF16)
        d_kv[:, vcols] = d_v.astype(BF16)


def back_kernel(
    index, d_query, d_kv, projection, point, mixed, inv, pre, hidden, tokens_t, *refs
):
    *outs, shifted, d_point, d_dil, piece = refs
    count = mixed.shape[0]
    narrow = pre.shape[1]
    d_normed = dot_t(d_query[...], projection[:, :KEY_COLS]) + dot_t(
        d_kv[...], projection[:, KEY_COLS:]
    )
    scale = inv[...]
    mix = mixed[...]
    pull = jnp.mean(d_normed * mix, axis=1, keepdims=True)
    d_mixed = (scale * d_normed - mix * (scale * scale * scale) * pull).astype(BF16)
    d_point[...] = lax.dot_general(
        hidden[...], d_mixed, (((0,), (0,)), ((), ())), preferred_element_type=F32
    )
    d_hidden = dot_t(d_mixed, point[...])
    x = pre[...]
    inner = jnp.tanh(GELU_C * (x + 0.044715 * (x * x * x)))
    slope = 0.5 * (1.0 + inner) + 0.5 * x * (1.0 - inner * inner) * (
        GELU_C * (1.0 + (3 * 0.044715) * (x * x))
    )
    d_pre = (d_hidden * slope).astype(BF16)
    shifted[...] = jnp.zeros_like(shifted)
    for tap in range(3):
        shifted[
            tap * DILATION_STEP : tap * DILATION_STEP + count, tap * narrow : (tap + 1) * narrow
        ] = d_pre
    d_dil[...] = dot(tokens_t[...], shifted[...])
    rows = d_dil.shape[0] // PIECES
    slim = d_point.shape[0] // PIECES
    full = d_dil.shape[1]
    rest = d_point.shape[1] - full
    for out_number, out in enumerate(outs):
        for k in range(out.shape[0]):
            place = index[out_number * out.shape[0] + k]
            piece[:rows, :] = d_dil[pl.ds(pl.multiple_of(place * rows, rows), rows), :]
            start = pl.multiple_of(place * slim, 8)
            piece[rows : rows + slim, :] = d_point[pl.ds(start, slim), :full]
            for j in range(slim // 8):
                piece[rows + slim :, j * rest : (j + 1) * rest] = d_point[
                    pl.ds(start + 8 * j, 8), full:
                ]
            out[k] = piece[...].astype(out.dtype)


def neighbours(value, count):
    return (
        lax.ppermute(value, "ctx", [(i, i + 1) for i in range(count - 1)]),
        lax.ppermute(value, "ctx", [(i + 1, i) for i in range(count - 1)]),
    )


def ring(step):
    return lambda value: lax.ppermute(
        value, "ctx", [(i, (i + step) % PIECES) for i in range(PIECES)]
    )


def swap(bit):
    return lambda value: lax.ppermute(value, "ctx", [(i, i ^ bit) for i in range(PIECES)])


UP, DOWN, ACROSS, CORE = ring(4), ring(-4), swap(2), swap(1)


def gathered(block):
    before, after = UP(block), DOWN(block)
    line = [block, after, UP(before), before]
    beside = [ACROSS(line[z]) for z in (0, 1, 3)]
    beside = [beside[0], beside[1], ACROSS(line[2]), beside[2]]
    mine = line + beside
    return mine + [CORE(value) for value in mine]


def relative_order():
    me = lax.axis_index("ctx")
    z, y, core = me // 4, (me // 2) % 2, me % 2
    order = []
    for d_core in range(2):
        for d_y in range(2):
            for d_z in range(4):
                y_part = y + d_y - 2 * y * d_y
                core_part = core + d_core - 2 * core * d_core
                order.append(((z + d_z) % 4) * 4 + y_part * 2 + core_part)
    return jnp.stack(order).astype(jnp.int32)


def unpack(total, narrow, model):
    rows, slim = total.shape[0] * 3 // 4, total.shape[0] * 3 // 16
    full = total.shape[1]
    rest = model - full
    tail = total[rows + slim :]
    tail = jnp.concatenate([tail[:, j * rest : (j + 1) * rest] for j in range(slim // 8)], axis=0)
    point = jnp.concatenate([total[rows : rows + slim], tail], axis=1)
    return total[:rows].reshape(rows, 3, narrow), point


def scattered(own_far, own_near, sent_far, sent_near):
    got_far = CORE(sent_far)
    got_near = CORE(sent_near)

    def across(z):
        return ACROSS((own_far[z] + got_far[z].astype(F32)).astype(BF16))

    order = {z: across(z) for z in (2, 1, 3, 0)}

    def held(z):
        return own_near[z] + got_near[z].astype(F32) + order[z].astype(F32)

    two = UP(held(2).astype(BF16))
    one = UP((held(1) + two.astype(F32)).astype(BF16))
    three = DOWN(held(3).astype(BF16))
    return held(0) + one.astype(F32) + three.astype(F32)


def body(
    count,
    tokens,
    dilated_weight,
    pointwise_weight,
    query_key_value_weight,
    slopes,
    chain_labels,
    attention_cotangent,
):
    rows, model = tokens.shape
    taps, narrow = dilated_weight.shape[1:]
    wide = taps * narrow
    columns = query_key_value_weight.shape[1]
    shard = model // PIECES
    slim = narrow // PIECES
    quick = count == PIECES

    before, after = neighbours(tokens[rows - DILATION_STEP :], count)[0], neighbours(
        tokens[:DILATION_STEP], count
    )[1]
    flat = dilated_weight.reshape(dilated_weight.shape[0], wide)

    def packed(projection, point):
        return jnp.concatenate(
            [projection]
            + [
                jnp.concatenate(
                    [point[:, j * narrow : (j + 1) * narrow] for j in range(model // narrow)],
                    axis=0,
                )
            ],
            axis=1,
        )

    if quick:
        conv_pieces = gathered(flat)
        rest_pieces = gathered(packed(query_key_value_weight, pointwise_weight))
        index = relative_order()
    else:
        all_flat = lax.all_gather(flat, "ctx", axis=0, tiled=True)
        all_point = lax.all_gather(pointwise_weight, "ctx", axis=0, tiled=True)
        all_projection = lax.all_gather(query_key_value_weight, "ctx", axis=0, tiled=True)
        conv_pieces = [all_flat[i * shard : (i + 1) * shard] for i in range(PIECES)]
        rest_pieces = [
            packed(
                all_projection[i * shard : (i + 1) * shard], all_point[i * slim : (i + 1) * slim]
            )
            for i in range(PIECES)
        ]
        index = jnp.arange(PIECES, dtype=jnp.int32)

    extended = jnp.concatenate([before, tokens, after], axis=0)
    tokens_t = extended.T

    start = lax.axis_index("ctx") * rows
    chain_pad = jnp.pad(chain_labels, (rows, rows), constant_values=-1)
    near_chain = lax.dynamic_slice_in_dim(chain_pad, start, 3 * rows)
    chain_rows = [near_chain[i * rows : (i + 1) * rows].reshape(1, rows) for i in range(3)]
    chain_column = near_chain[rows : 2 * rows].reshape(rows, 1)

    pre, hidden = pl.pallas_call(
        conv_kernel,
        out_shape=(
            jax.ShapeDtypeStruct((rows, narrow), F32),
            jax.ShapeDtypeStruct((rows, narrow), BF16),
        ),
        in_specs=[SMEM, VMEM] + [ANY] * PIECES,
        out_specs=(VMEM, VMEM),
        scratch_shapes=[
            pltpu.VMEM((model, wide), BF16),
            pltpu.SemaphoreType.DMA((PIECES,)),
        ],
        compiler_params=params(32),
        name="conv",
    )(index, extended, *conv_pieces)

    mixed, inv, qkv, projection, point = pl.pallas_call(
        project_kernel,
        out_shape=(
            jax.ShapeDtypeStruct((rows, model), F32),
            jax.ShapeDtypeStruct((rows, 1), F32),
            jax.ShapeDtypeStruct((rows, columns), BF16),
            jax.ShapeDtypeStruct((model, columns), BF16),
            jax.ShapeDtypeStruct((narrow, model), BF16),
        ),
        in_specs=[SMEM, VMEM, VMEM] + [ANY] * PIECES,
        out_specs=(VMEM,) * 5,
        scratch_shapes=[
            pltpu.VMEM((PIECES, shard, narrow), BF16),
            pltpu.VMEM((narrow, model), F32),
            pltpu.SemaphoreType.DMA((2, PIECES)),
        ],
        compiler_params=params(40),
        name="project",
    )(index, extended, hidden, *rest_pieces)

    query, kv = qkv[:, :KEY_COLS], qkv[:, KEY_COLS:]
    kv_prev, kv_next = neighbours(kv, count)
    q_prev, q_next = neighbours(query, count)
    d_prev, d_next = neighbours(attention_cotangent, count)

    attended, d_query, stats = pl.pallas_call(
        attend_kernel,
        out_shape=(
            jax.ShapeDtypeStruct((rows, HEADS * VAL), BF16),
            jax.ShapeDtypeStruct((rows, KEY_COLS), BF16),
            jax.ShapeDtypeStruct((2 * HEADS, rows), F32),
        ),
        in_specs=[SMEM] + [VMEM] * 9,
        out_specs=(VMEM,) * 3,
        compiler_params=params(40),
        name="attend",
    )(slopes, query, kv_prev, kv, kv_next, attention_cotangent, chain_column, *chain_rows)

    s_prev, s_next = neighbours(stats, count)
    groups = [
        (q_prev, d_prev, s_prev, s_prev, chain_rows[0]),
        (query, attention_cotangent, stats, stats, chain_rows[1]),
        (q_next, d_next, s_next, s_next, chain_rows[2]),
    ]
    d_kv = pl.pallas_call(
        key_grad_kernel,
        out_shape=jax.ShapeDtypeStruct(kv.shape, BF16),
        in_specs=[SMEM] + [VMEM] * 17,
        out_specs=VMEM,
        compiler_params=params(40),
        name="key_grad",
    )(slopes, kv, chain_column, *[ref for group in groups for ref in group])

    piece = (shard + 2 * slim * 2 // 3, wide)
    if quick:
        quarter = (4,) + piece
        shapes = [
            jax.ShapeDtypeStruct(quarter, kind) for kind in (F32, F32, BF16, BF16)
        ]
    else:
        shapes = [jax.ShapeDtypeStruct((PIECES,) + piece, F32)]
    outs = pl.pallas_call(
        back_kernel,
        out_shape=tuple(shapes),
        in_specs=[SMEM] + [VMEM] * 9,
        out_specs=(VMEM,) * len(shapes),
        scratch_shapes=[
            pltpu.VMEM((rows + 2 * DILATION_STEP, wide), BF16),
            pltpu.VMEM((narrow, model), F32),
            pltpu.VMEM((model, wide), F32),
            pltpu.VMEM(piece, F32),
        ],
        compiler_params=params(56),
        name="back",
    )(index, d_query, d_kv, projection, point, mixed, inv, pre, hidden, tokens_t)

    if quick:
        own_near, own_far, sent_near, sent_far = outs
        total = scattered(own_far, own_near, sent_far, sent_near)
        dilated_grad, point_grad = unpack(total, narrow, model)
    else:
        parts = [unpack(outs[0][i], narrow, model) for i in range(PIECES)]
        dilated_grad, point_grad = (
            lax.psum_scatter(
                jnp.concatenate([part[k] for part in parts], axis=0),
                "ctx",
                scatter_dimension=0,
                tiled=True,
            )
            for k in range(2)
        )
    return (attended, dilated_grad, point_grad)


def solution(mesh):
    return jax.shard_map(
        functools.partial(body, mesh.shape["ctx"]),
        mesh=mesh,
        in_specs=(
            P(("groups", "ctx"), None),
            P("ctx", None, None),
            P("ctx", None),
            P("ctx", None),
            P(),
            P("groups"),
            P(("groups", "ctx"), None),
        ),
        out_specs=(
            P(("groups", "ctx"), None),
            P(("groups", "ctx"), None, None),
            P(("groups", "ctx"), None),
        ),
        check_vma=False,
    )
```

```python
import functools
import math

import jax
import jax.numpy as jnp
from jax import lax
from jax.experimental import pallas as pl
from jax.experimental.pallas import tpu as pltpu
from jax.sharding import PartitionSpec as P

HEADS = 4
KEY = 64
VAL = 192
DILATION_STEP = 16
KEY_COLS = HEADS * KEY
NEG_FILL = -1e30
SCALE = 1.0 / math.sqrt(KEY)
GELU_C = math.sqrt(2.0 / math.pi)
PIECES = 16

F32 = jnp.float32
BF16 = jnp.bfloat16
VMEM = pl.BlockSpec(memory_space=pltpu.VMEM)
SMEM = pl.BlockSpec(memory_space=pltpu.SMEM)
HBM = pl.BlockSpec(memory_space=pltpu.HBM)


def dot(a, b):
    return jnp.dot(a, b, preferred_element_type=F32)


def dot_t(a, b):
    return lax.dot_general(a, b, (((1,), (1,)), ((), ())), preferred_element_type=F32)


def params(mib):
    return pltpu.CompilerParams(vmem_limit_bytes=mib << 20)


def extend_kernel(before, tokens, after, extended, extended_t):
    step, rows = before.shape[0], tokens.shape[0]
    extended[:step, :] = before[...]
    extended[step : step + rows, :] = tokens[...]
    extended[step + rows :, :] = after[...]
    extended_t[...] = extended[...].astype(F32).T.astype(BF16)


def conv_kernel(index, tokens, *refs):
    pieces, (pre, hidden, weight, sems) = refs[:PIECES], refs[PIECES:]
    rows = pieces[0].shape[0]
    copies = []
    for i, piece in enumerate(pieces):
        start = pl.multiple_of(index[i] * rows, rows)
        copies.append(pltpu.make_async_copy(piece, weight.at[pl.ds(start, rows)], sems.at[i]))
    for copy in copies:
        copy.start()
    for copy in copies:
        copy.wait()
    count, narrow = pre.shape
    total = None
    for tap in range(3):
        part = dot(
            tokens[tap * DILATION_STEP : tap * DILATION_STEP + count, :],
            weight[:, tap * narrow : (tap + 1) * narrow],
        )
        total = part if total is None else total + part
    pre[...] = total
    inner = jnp.tanh(GELU_C * (total + 0.044715 * (total * total * total)))
    hidden[...] = (total * (0.5 * (1.0 + inner))).astype(BF16)


def project_kernel(index, tokens, hidden, *refs):
    pieces = refs[:PIECES]
    mixed, inv, qkv, projection, point, blocks, wide, sems = refs[PIECES:]
    rows = pieces[0].shape[0]
    columns = projection.shape[1]
    count = mixed.shape[0]
    copies = []
    for i, piece in enumerate(pieces):
        start = pl.multiple_of(index[i] * rows, rows)
        copies.append(
            pltpu.make_async_copy(
                piece.at[:, columns:], blocks.at[i], sems.at[0, i]
            )
        )
        copies.append(
            pltpu.make_async_copy(
                piece.at[:, :columns], projection.at[pl.ds(start, rows)], sems.at[1, i]
            )
        )
    for copy in copies:
        copy.start()
    for copy in copies[::2]:
        copy.wait()
    slim = rows // 4
    width = blocks.shape[2]
    for i in range(PIECES):
        block = blocks[i].astype(F32)
        start = pl.multiple_of(index[i] * slim, 8)
        for j in range(4):
            wide[pl.ds(start, slim), j * width : (j + 1) * width] = block[
                j * slim : (j + 1) * slim
            ]
    point[...] = wide[...].astype(BF16)
    mix = tokens[DILATION_STEP : DILATION_STEP + count, :].astype(F32) + dot(
        hidden[...], point[...]
    )
    mixed[...] = mix
    scale = lax.rsqrt(jnp.mean(mix * mix, axis=1, keepdims=True) + 1e-06)
    inv[...] = scale
    normed = (mix * scale).astype(BF16)
    for copy in copies[1::2]:
        copy.wait()
    qkv[...] = dot(normed, projection[...]).astype(BF16)


def distance(shape, shift):
    a = lax.broadcasted_iota(jnp.int32, shape, 0)
    b = lax.broadcasted_iota(jnp.int32, shape, 1)
    return jnp.abs(a - b + shift).astype(F32)


def attend_kernel(
    slopes, query, kv_prev, kv, kv_next, d_out, q_chain, k_prev, k_own, k_next, *refs
):
    attended, d_query, stats = refs
    count = query.shape[0]
    near = (kv_prev, kv, kv_next)
    away = [distance((count, count), shift) for shift in (count, 0, -count)]
    same = [q_chain[...] == chain[...] for chain in (k_prev, k_own, k_next)]
    tops, deltas = [], []
    for head in range(HEADS):
        kcols = slice(head * KEY, (head + 1) * KEY)
        vcols = slice(KEY_COLS + head * VAL, KEY_COLS + (head + 1) * VAL)
        ocols = slice(head * VAL, (head + 1) * VAL)
        q = query[:, kcols]
        slope = slopes[head]
        scores = []
        for i in range(3):
            score = dot_t(q, near[i][:, kcols]) * SCALE - slope * away[i]
            scores.append(jnp.where(same[i], score, NEG_FILL))
        top = functools.reduce(
            jnp.maximum, [jnp.max(s, axis=1, keepdims=True) for s in scores]
        )
        expo = [jnp.exp(s - top) for s in scores]
        denom = sum(jnp.sum(e, axis=1, keepdims=True) for e in expo)
        share = 1.0 / denom
        prob = [e * share for e in expo]
        out = sum(dot(p.astype(BF16), near[i][:, vcols]) for i, p in enumerate(prob))
        attended[:, ocols] = out.astype(BF16)
        d_head = d_out[:, ocols]
        delta = jnp.sum(d_head.astype(F32) * out, axis=1, keepdims=True)
        d_q = None
        for i in range(3):
            d_prob = dot_t(d_head, near[i][:, vcols])
            d_score = (prob[i] * (d_prob - delta) * SCALE).astype(BF16)
            part = dot(d_score, near[i][:, kcols])
            d_q = part if d_q is None else d_q + part
        d_query[:, kcols] = d_q.astype(BF16)
        tops.append(top + jnp.log(denom))
        deltas.append(delta)
    pad = jnp.zeros((count, 128 - 2 * HEADS), F32)
    packed = jnp.concatenate(tops + deltas + [pad], axis=1)
    stats[...] = packed.T[: 2 * HEADS]


def key_grad_kernel(slopes, kv, k_chain, *refs):
    groups, (d_kv,) = [refs[5 * i : 5 * i + 5] for i in range(3)], refs[15:]
    count = kv.shape[0]
    away = [distance((count, count), shift) for shift in (count, 0, -count)]
    same = [k_chain[...] == group[4][...] for group in groups]
    for head in range(HEADS):
        kcols = slice(head * KEY, (head + 1) * KEY)
        vcols = slice(KEY_COLS + head * VAL, KEY_COLS + (head + 1) * VAL)
        ocols = slice(head * VAL, (head + 1) * VAL)
        k, v, slope = kv[:, kcols], kv[:, vcols], slopes[head]
        d_k = d_v = None
        for i, (query, d_out, stats, _, _) in enumerate(groups):
            q, d_head = query[:, kcols], d_out[:, ocols]
            score = dot_t(k, q) * SCALE - slope * away[i]
            score = jnp.where(same[i], score, NEG_FILL)
            back = jnp.exp(score - stats[head : head + 1, :])
            d_prob = dot_t(v, d_head)
            d_score = back * (d_prob - stats[HEADS + head : HEADS + head + 1, :]) * SCALE
            part_k, part_v = dot(d_score.astype(BF16), q), dot(back.astype(BF16), d_head)
            d_k = part_k if d_k is None else d_k + part_k
            d_v = part_v if d_v is None else d_v + part_v
        d_kv[:, kcols] = d_k.astype(BF16)
        d_kv[:, vcols] = d_v.astype(BF16)


def back_kernel(
    index, d_query, d_kv, projection, point, mixed, inv, pre, hidden, tokens_t, *refs
):
    *outs, shifted, d_point, d_dil, piece = refs
    count = mixed.shape[0]
    narrow = pre.shape[1]
    d_normed = dot_t(d_query[...], projection[:, :KEY_COLS]) + dot_t(
        d_kv[...], projection[:, KEY_COLS:]
    )
    scale = inv[...]
    mix = mixed[...]
    pull = jnp.mean(d_normed * mix, axis=1, keepdims=True)
    d_mixed = (scale * d_normed - mix * (scale * scale * scale) * pull).astype(BF16)
    d_point[...] = lax.dot_general(
        hidden[...], d_mixed, (((0,), (0,)), ((), ())), preferred_element_type=F32
    )
    d_hidden = dot_t(d_mixed, point[...])
    x = pre[...]
    inner = jnp.tanh(GELU_C * (x + 0.044715 * (x * x * x)))
    slope = 0.5 * (1.0 + inner) + 0.5 * x * (1.0 - inner * inner) * (
        GELU_C * (1.0 + (3 * 0.044715) * (x * x))
    )
    d_pre = (d_hidden * slope).astype(BF16)
    shifted[...] = jnp.zeros_like(shifted)
    for tap in range(3):
        shifted[
            tap * DILATION_STEP : tap * DILATION_STEP + count, tap * narrow : (tap + 1) * narrow
        ] = d_pre
    d_dil[...] = dot(tokens_t[...], shifted[...])
    rows = d_dil.shape[0] // PIECES
    slim = d_point.shape[0] // PIECES
    full = d_dil.shape[1]
    rest = d_point.shape[1] - full
    for out_number, out in enumerate(outs):
        for k in range(out.shape[0]):
            place = index[out_number * out.shape[0] + k]
            piece[:rows, :] = d_dil[pl.ds(pl.multiple_of(place * rows, rows), rows), :]
            start = pl.multiple_of(place * slim, 8)
            piece[rows : rows + slim, :] = d_point[pl.ds(start, slim), :full]
            for j in range(slim // 8):
                piece[rows + slim :, j * rest : (j + 1) * rest] = d_point[
                    pl.ds(start + 8 * j, 8), full:
                ]
            out[k] = piece[...].astype(out.dtype)


def neighbours(value, count):
    return (
        lax.ppermute(value, "ctx", [(i, i + 1) for i in range(count - 1)]),
        lax.ppermute(value, "ctx", [(i + 1, i) for i in range(count - 1)]),
    )


def ring(step):
    return lambda value: lax.ppermute(
        value, "ctx", [(i, (i + step) % PIECES) for i in range(PIECES)]
    )


def swap(bit):
    return lambda value: lax.ppermute(value, "ctx", [(i, i ^ bit) for i in range(PIECES)])


UP, DOWN, ACROSS, CORE = ring(4), ring(-4), swap(2), swap(1)


def other_group(value):
    return lax.ppermute(value, "groups", [(0, 1), (1, 0)])


def gathered(block):
    first = lax.axis_index("groups") == 0
    below, above = UP(block), DOWN(block)
    two = UP(below)
    beside = [
        ACROSS(jnp.where(first, block, above)),
        ACROSS(jnp.where(first, below, two)),
    ]
    passed = [other_group(value) for value in beside]
    mine = [block, above, two, below, beside[0], passed[0], beside[1], passed[1]]
    return mine + [CORE(value) for value in mine], (below, above), beside[1]


def place(me, d_core, d_y, d_z):
    z, y, core = me // 4, (me // 2) % 2, me % 2
    y, core = y + d_y - 2 * y * d_y, core + d_core - 2 * core * d_core
    return ((z + d_z) % 4) * 4 + y * 2 + core


def piece_order():
    me, group = lax.axis_index("ctx"), lax.axis_index("groups")
    order = []
    for d_core in range(2):
        order += [place(me, d_core, 0, d_z) for d_z in range(4)]
        order += [
            place(me, d_core, 1, d_z) for d_z in (group, 1 - group, 3 - group, 2 + group)
        ]
    return jnp.stack(order).astype(jnp.int32)


def relative_order():
    me = lax.axis_index("ctx")
    order = [place(me, c, y, z) for c in range(2) for y in range(2) for z in range(4)]
    return jnp.stack(order).astype(jnp.int32)


def unpack(total, narrow, model):
    rows, slim = total.shape[0] * 3 // 4, total.shape[0] * 3 // 16
    full = total.shape[1]
    rest = model - full
    tail = total[rows + slim :]
    tail = jnp.concatenate([tail[:, j * rest : (j + 1) * rest] for j in range(slim // 8)], axis=0)
    point = jnp.concatenate([total[rows : rows + slim], tail], axis=1)
    return total[:rows].reshape(rows, 3, narrow), point


def scattered(own_far, own_near, sent_far, sent_near):
    got_far = CORE(sent_far)
    got_near = CORE(sent_near)

    def across(z):
        return ACROSS((own_far[z] + got_far[z].astype(F32)).astype(BF16))

    order = {z: across(z) for z in (2, 1, 3, 0)}

    def held(z):
        return own_near[z] + got_near[z].astype(F32) + order[z].astype(F32)

    two = UP(held(2).astype(BF16))
    one = UP((held(1) + two.astype(F32)).astype(BF16))
    three = DOWN(held(3).astype(BF16))
    return held(0) + one.astype(F32) + three.astype(F32)


def body(
    count,
    tokens,
    dilated_weight,
    pointwise_weight,
    query_key_value_weight,
    slopes,
    chain_labels,
    attention_cotangent,
):
    rows, model = tokens.shape
    taps, narrow = dilated_weight.shape[1:]
    wide = taps * narrow
    columns = query_key_value_weight.shape[1]
    shard = model // PIECES
    slim = narrow // PIECES
    quick = count == PIECES

    before, after = neighbours(tokens[rows - DILATION_STEP :], count)[0], neighbours(
        tokens[:DILATION_STEP], count
    )[1]
    flat = dilated_weight.reshape(dilated_weight.shape[0], wide)

    def packed(projection, point):
        return jnp.concatenate(
            [projection]
            + [
                jnp.concatenate(
                    [point[:, j * narrow : (j + 1) * narrow] for j in range(model // narrow)],
                    axis=0,
                )
            ],
            axis=1,
        )

    if quick:
        conv_pieces, step, _ = gathered(flat)
        rest, _ = lax.optimization_barrier(
            (packed(query_key_value_weight, pointwise_weight), step)
        )
        rest_pieces, _, late = gathered(rest)
        cotangent, _ = lax.optimization_barrier((attention_cotangent, late))
        index, relative = piece_order(), relative_order()
    else:
        all_flat = lax.all_gather(flat, "ctx", axis=0, tiled=True)
        all_point = lax.all_gather(pointwise_weight, "ctx", axis=0, tiled=True)
        all_projection = lax.all_gather(query_key_value_weight, "ctx", axis=0, tiled=True)
        conv_pieces = [all_flat[i * shard : (i + 1) * shard] for i in range(PIECES)]
        rest_pieces = [
            packed(
                all_projection[i * shard : (i + 1) * shard], all_point[i * slim : (i + 1) * slim]
            )
            for i in range(PIECES)
        ]
        index = relative = jnp.arange(PIECES, dtype=jnp.int32)
        cotangent = attention_cotangent

    span = rows + 2 * DILATION_STEP
    extended, tokens_t = pl.pallas_call(
        extend_kernel,
        out_shape=(
            jax.ShapeDtypeStruct((span, model), BF16),
            jax.ShapeDtypeStruct((model, span), BF16),
        ),
        in_specs=[VMEM] * 3,
        out_specs=(VMEM, VMEM),
        compiler_params=params(10),
        name="extend",
    )(before, tokens, after)

    start = lax.axis_index("ctx") * rows
    chain_pad = jnp.pad(chain_labels, (rows, rows), constant_values=-1)
    near_chain = lax.dynamic_slice_in_dim(chain_pad, start, 3 * rows)
    chain_rows = [near_chain[i * rows : (i + 1) * rows].reshape(1, rows) for i in range(3)]
    chain_column = near_chain[rows : 2 * rows].reshape(rows, 1)

    pre, hidden = pl.pallas_call(
        conv_kernel,
        out_shape=(
            jax.ShapeDtypeStruct((rows, narrow), F32),
            jax.ShapeDtypeStruct((rows, narrow), BF16),
        ),
        in_specs=[SMEM, VMEM] + [HBM] * PIECES,
        out_specs=(VMEM, VMEM),
        scratch_shapes=[
            pltpu.VMEM((model, wide), BF16),
            pltpu.SemaphoreType.DMA((PIECES,)),
        ],
        compiler_params=params(14),
        name="conv",
    )(index, extended, *conv_pieces)

    mixed, inv, qkv, projection, point = pl.pallas_call(
        project_kernel,
        out_shape=(
            jax.ShapeDtypeStruct((rows, model), F32),
            jax.ShapeDtypeStruct((rows, 1), F32),
            jax.ShapeDtypeStruct((rows, columns), BF16),
            jax.ShapeDtypeStruct((model, columns), BF16),
            jax.ShapeDtypeStruct((narrow, model), BF16),
        ),
        in_specs=[SMEM, VMEM, VMEM] + [HBM] * PIECES,
        out_specs=(VMEM,) * 5,
        scratch_shapes=[
            pltpu.VMEM((PIECES, shard, narrow), BF16),
            pltpu.VMEM((narrow, model), F32),
            pltpu.SemaphoreType.DMA((2, PIECES)),
        ],
        compiler_params=params(24),
        name="project",
    )(index, extended, hidden, *rest_pieces)

    query, kv = qkv[:, :KEY_COLS], qkv[:, KEY_COLS:]
    d_prev, d_next = neighbours(cotangent, count)
    kv, d_prev, d_next = lax.optimization_barrier((kv, d_prev, d_next))
    kv_prev, kv_next = neighbours(kv, count)
    later, kv_prev, kv_next = lax.optimization_barrier((query, kv_prev, kv_next))
    q_prev, q_next = neighbours(later, count)

    attended, d_query, stats = pl.pallas_call(
        attend_kernel,
        out_shape=(
            jax.ShapeDtypeStruct((rows, HEADS * VAL), BF16),
            jax.ShapeDtypeStruct((rows, KEY_COLS), BF16),
            jax.ShapeDtypeStruct((2 * HEADS, rows), F32),
        ),
        in_specs=[SMEM] + [VMEM] * 9,
        out_specs=(VMEM,) * 3,
        compiler_params=params(20),
        name="attend",
    )(slopes, query, kv_prev, kv, kv_next, attention_cotangent, chain_column, *chain_rows)

    s_prev, s_next = neighbours(stats, count)
    groups = [
        (q_prev, d_prev, s_prev, s_prev, chain_rows[0]),
        (query, attention_cotangent, stats, stats, chain_rows[1]),
        (q_next, d_next, s_next, s_next, chain_rows[2]),
    ]
    d_kv = pl.pallas_call(
        key_grad_kernel,
        out_shape=jax.ShapeDtypeStruct(kv.shape, BF16),
        in_specs=[SMEM] + [VMEM] * 17,
        out_specs=VMEM,
        compiler_params=params(16),
        name="key_grad",
    )(slopes, kv, chain_column, *[ref for group in groups for ref in group])

    piece = (shard + 2 * slim * 2 // 3, wide)
    if quick:
        quarter = (4,) + piece
        shapes = [
            jax.ShapeDtypeStruct(quarter, kind) for kind in (F32, F32, BF16, BF16)
        ]
    else:
        shapes = [jax.ShapeDtypeStruct((PIECES,) + piece, F32)]
    outs = pl.pallas_call(
        back_kernel,
        out_shape=tuple(shapes),
        in_specs=[SMEM] + [VMEM] * 9,
        out_specs=(VMEM,) * len(shapes),
        scratch_shapes=[
            pltpu.VMEM((rows + 2 * DILATION_STEP, wide), BF16),
            pltpu.VMEM((narrow, model), F32),
            pltpu.VMEM((model, wide), F32),
            pltpu.VMEM(piece, F32),
        ],
        compiler_params=params(40),
        name="back",
    )(relative, d_query, d_kv, projection, point, mixed, inv, pre, hidden, tokens_t)

    if quick:
        own_near, own_far, sent_near, sent_far = outs
        total = scattered(own_far, own_near, sent_far, sent_near)
        dilated_grad, point_grad = unpack(total, narrow, model)
    else:
        parts = [unpack(outs[0][i], narrow, model) for i in range(PIECES)]
        dilated_grad, point_grad = (
            lax.psum_scatter(
                jnp.concatenate([part[k] for part in parts], axis=0),
                "ctx",
                scatter_dimension=0,
                tiled=True,
            )
            for k in range(2)
        )
    return (attended, dilated_grad, point_grad)


def solution(mesh):
    return jax.shard_map(
        functools.partial(body, mesh.shape["ctx"]),
        mesh=mesh,
        in_specs=(
            P(("groups", "ctx"), None),
            P("ctx", None, None),
            P("ctx", None),
            P("ctx", None),
            P(),
            P("groups"),
            P(("groups", "ctx"), None),
        ),
        out_specs=(
            P(("groups", "ctx"), None),
            P(("groups", "ctx"), None, None),
            P(("groups", "ctx"), None),
        ),
        check_vma=False,
    )
```

```python
import functools
import math

import jax
import jax.numpy as jnp
from jax import lax
from jax.experimental import pallas as pl
from jax.experimental.pallas import tpu as pltpu
from jax.sharding import PartitionSpec as P

HEADS = 4
KEY = 64
VAL = 192
DILATION_STEP = 16
KEY_COLS = HEADS * KEY
FAR = 1e33
SCALE = 1.0 / math.sqrt(KEY)
GELU_C = math.sqrt(2.0 / math.pi)
PIECES = 16
LATE = 8

F32 = jnp.float32
BF16 = jnp.bfloat16
VMEM = pl.BlockSpec(memory_space=pltpu.VMEM)
SMEM = pl.BlockSpec(memory_space=pltpu.SMEM)
HBM = pl.BlockSpec(memory_space=pltpu.HBM)


def dot(a, b):
    return jnp.dot(a, b, preferred_element_type=F32)


def dot_t(a, b):
    return lax.dot_general(a, b, (((1,), (1,)), ((), ())), preferred_element_type=F32)


def in_hbm(value):
    return pltpu.with_memory_space_constraint(value, pltpu.HBM)


def params(mib):
    return pltpu.CompilerParams(vmem_limit_bytes=mib << 20)


def extend_kernel(order, before, tokens, after, extended, *refs):
    *halves, turned = refs
    step, rows = before.shape[0], tokens.shape[0]
    extended[:step, :] = before[...]
    extended[step : step + rows, :] = tokens[...]
    extended[step + rows :, :] = after[...]
    turned[...] = extended[...].astype(F32).T.astype(BF16)
    shard = turned.shape[0] // PIECES
    for i in range(PIECES):
        start = pl.multiple_of(order[i] * shard, shard)
        half, k = halves[i // 8], i % 8
        half[k * shard : (k + 1) * shard, :] = turned[pl.ds(start, shard), :]


def conv_kernel(index, tokens, *refs):
    pieces, (pre, hidden, weight, sems) = refs[:PIECES], refs[PIECES:]
    rows = pieces[0].shape[0]
    copies = []
    for i, piece in enumerate(pieces):
        start = pl.multiple_of(index[i] * rows, rows)
        copies.append(pltpu.make_async_copy(piece, weight.at[pl.ds(start, rows)], sems.at[i]))
    for copy in copies:
        copy.start()
    for copy in copies:
        copy.wait()
    count, narrow = pre.shape
    total = None
    for tap in range(3):
        part = dot(
            tokens[tap * DILATION_STEP : tap * DILATION_STEP + count, :],
            weight[:, tap * narrow : (tap + 1) * narrow],
        )
        total = part if total is None else total + part
    pre[...] = total
    inner = jnp.tanh(GELU_C * (total + 0.044715 * (total * total * total)))
    hidden[...] = (total * (0.5 * (1.0 + inner))).astype(BF16)


def project_kernel(index, tokens, hidden, *refs):
    pieces = refs[:PIECES]
    mixed, inv, query, kv, projection, point, blocks, wide, sems = refs[PIECES:]
    rows = pieces[0].shape[0]
    columns = projection.shape[1]
    count = mixed.shape[0]
    copies = []
    for i, piece in enumerate(pieces):
        start = pl.multiple_of(index[i] * rows, rows)
        copies.append(
            pltpu.make_async_copy(
                piece.at[:, columns:], blocks.at[i], sems.at[0, i]
            )
        )
        copies.append(
            pltpu.make_async_copy(
                piece.at[:, :columns], projection.at[pl.ds(start, rows)], sems.at[1, i]
            )
        )
    for copy in copies:
        copy.start()
    for copy in copies[::2]:
        copy.wait()
    slim = rows // 4
    width = blocks.shape[2]
    for i in range(PIECES):
        block = blocks[i].astype(F32)
        start = pl.multiple_of(index[i] * slim, 8)
        for j in range(4):
            wide[pl.ds(start, slim), j * width : (j + 1) * width] = block[
                j * slim : (j + 1) * slim
            ]
    point[...] = wide[...].astype(BF16)
    mix = tokens[DILATION_STEP : DILATION_STEP + count, :].astype(F32) + dot(
        hidden[...], point[...]
    )
    mixed[...] = mix
    scale = lax.rsqrt(jnp.mean(mix * mix, axis=1, keepdims=True) + 1e-06)
    inv[...] = scale
    normed = (mix * scale).astype(BF16)
    for copy in copies[1::2]:
        copy.wait()
    kv[...] = dot(normed, projection[:, KEY_COLS:]).astype(BF16)
    query[...] = dot(normed, projection[:, :KEY_COLS]).astype(BF16)


def distance(shape, shift):
    a = lax.broadcasted_iota(jnp.int32, shape, 0)
    b = lax.broadcasted_iota(jnp.int32, shape, 1)
    return jnp.abs(a - b + shift).astype(F32)


def masked_distance(same, shift):
    return jnp.where(same, distance(same.shape, shift), FAR)


def attend_kernel(
    slopes, query, kv_prev, kv, kv_next, d_out, q_chain, k_prev, k_own, k_next, *refs
):
    attended, d_query, stats, before, after, sems = refs
    copies = [
        pltpu.make_async_copy(kv_prev, before, sems.at[0]),
        pltpu.make_async_copy(kv_next, after, sems.at[1]),
    ]
    for copy in copies:
        copy.start()
    count = query.shape[0]
    near = (before, kv, after)
    away = [
        masked_distance(q_chain[...] == chain[...], shift)
        for chain, shift in ((k_prev, count), (k_own, 0), (k_next, -count))
    ]
    for copy in copies:
        copy.wait()
    tops, deltas = [], []
    for head in range(HEADS):
        kcols = slice(head * KEY, (head + 1) * KEY)
        vcols = slice(KEY_COLS + head * VAL, KEY_COLS + (head + 1) * VAL)
        ocols = slice(head * VAL, (head + 1) * VAL)
        q = query[:, kcols] * SCALE
        slope = slopes[head]
        scores = [dot_t(q, near[i][:, kcols]) - slope * away[i] for i in range(3)]
        top = jnp.max(
            functools.reduce(jnp.maximum, scores), axis=1, keepdims=True
        )
        expo = [jnp.exp(s - top) for s in scores]
        denom = jnp.sum(expo[0] + expo[1] + expo[2], axis=1, keepdims=True)
        share = 1.0 / denom
        prob = [e * share for e in expo]
        out = sum(dot(p.astype(BF16), near[i][:, vcols]) for i, p in enumerate(prob))
        attended[:, ocols] = out.astype(BF16)
        d_head = d_out[:, ocols]
        delta = jnp.sum(d_head.astype(F32) * out, axis=1, keepdims=True)
        d_q = None
        for i in range(3):
            d_prob = dot_t(d_head, near[i][:, vcols])
            d_score = (prob[i] * (d_prob - delta)).astype(BF16)
            part = dot(d_score, near[i][:, kcols])
            d_q = part if d_q is None else d_q + part
        d_query[:, kcols] = (d_q * SCALE).astype(BF16)
        tops.append(top + jnp.log(denom))
        deltas.append(delta)
    pad = jnp.zeros((count, 128 - 2 * HEADS), F32)
    packed = jnp.concatenate(tops + deltas + [pad], axis=1)
    stats[...] = packed.T[: 2 * HEADS]


def key_grad_kernel(shifts, slopes, kv, k_chain, *refs):
    groups = [refs[4 * i : 4 * i + 4] for i in range(len(shifts))]
    more, d_kv = refs[4 * len(shifts) : -1], refs[-1]
    count = kv.shape[0]
    away = [
        masked_distance(k_chain[...] == group[3][...], shift * count)
        for group, shift in zip(groups, shifts)
    ]
    for head in range(HEADS):
        kcols = slice(head * KEY, (head + 1) * KEY)
        vcols = slice(KEY_COLS + head * VAL, KEY_COLS + (head + 1) * VAL)
        ocols = slice(head * VAL, (head + 1) * VAL)
        k, v, slope = kv[:, kcols] * SCALE, kv[:, vcols], slopes[head]
        d_k = d_v = None
        for i, (query, d_out, stats, _) in enumerate(groups):
            q, d_head = query[:, kcols], d_out[:, ocols]
            score = dot_t(k, q) - slope * away[i]
            back = jnp.exp(score - stats[head : head + 1, :])
            d_prob = dot_t(v, d_head)
            d_score = back * (d_prob - stats[HEADS + head : HEADS + head + 1, :])
            part_k, part_v = dot(d_score.astype(BF16), q), dot(back.astype(BF16), d_head)
            d_k = part_k if d_k is None else d_k + part_k
            d_v = part_v if d_v is None else d_v + part_v
        d_k = d_k * SCALE
        if more:
            d_k, d_v = d_k + more[0][:, kcols], d_v + more[0][:, vcols]
        d_kv[:, kcols] = d_k.astype(d_kv.dtype)
        d_kv[:, vcols] = d_v.astype(d_kv.dtype)


def mix_back_kernel(index, d_query, d_kv, projection, mixed, inv, hidden, d_mixed, *refs):
    *outs, d_point = refs
    d_normed = dot_t(d_query[...], projection[:, :KEY_COLS]) + dot_t(
        d_kv[...], projection[:, KEY_COLS:]
    )
    scale = inv[...]
    mix = mixed[...]
    pull = jnp.mean(d_normed * mix, axis=1, keepdims=True)
    grad = (scale * d_normed - mix * (scale * scale * scale) * pull).astype(BF16)
    d_mixed[...] = grad
    d_point[...] = lax.dot_general(
        hidden[...], grad, (((0,), (0,)), ((), ())), preferred_element_type=F32
    )
    slim = d_point.shape[0] // PIECES
    full = outs[0].shape[2]
    rest = d_point.shape[1] - full
    for number in range(PIECES):
        out, k = outs[number // 8], number % 8
        start = pl.multiple_of(index[number] * slim, 8)
        out[k, :slim, :] = d_point[pl.ds(start, slim), :full]
        for j in range(slim // 8):
            out[k, slim:, j * rest : (j + 1) * rest] = d_point[pl.ds(start + 8 * j, 8), full:]


def put(value, point, outs):
    rows = value.shape[0] // 8
    for i, out in enumerate(outs):
        for k in range(out.shape[0]):
            number = i * out.shape[0] + k
            out[k, :rows, :] = value[number * rows : (number + 1) * rows].astype(out.dtype)
            out[k, rows:, :] = point[number].astype(out.dtype)


def conv_back_kernel(d_mixed, point, pre, tokens_t, d_point, shifted, *outs):
    count, narrow = pre.shape
    d_hidden = dot_t(d_mixed[...], point[...])
    x = pre[...]
    inner = jnp.tanh(GELU_C * (x + 0.044715 * (x * x * x)))
    slope = 0.5 * (1.0 + inner) + 0.5 * x * (1.0 - inner * inner) * (
        GELU_C * (1.0 + (3 * 0.044715) * (x * x))
    )
    d_pre = (d_hidden * slope).astype(BF16)
    shifted[...] = jnp.zeros_like(shifted)
    for tap in range(3):
        shifted[
            tap * DILATION_STEP : tap * DILATION_STEP + count, tap * narrow : (tap + 1) * narrow
        ] = d_pre
    put(dot(tokens_t[...], shifted[...]), d_point, outs)


def conv_own_kernel(shifted, tokens_t, d_point, *outs):
    put(dot(tokens_t[...], shifted[...]), d_point, outs)


def neighbours(value, count):
    return (
        lax.ppermute(value, "ctx", [(i, i + 1) for i in range(count - 1)]),
        lax.ppermute(value, "ctx", [(i + 1, i) for i in range(count - 1)]),
    )


def ring(step):
    return lambda value: lax.ppermute(
        value, "ctx", [(i, (i + step) % PIECES) for i in range(PIECES)]
    )


def swap(bit):
    return lambda value: lax.ppermute(value, "ctx", [(i, i ^ bit) for i in range(PIECES)])


UP, DOWN, ACROSS, CORE = ring(4), ring(-4), swap(2), swap(1)


def other_group(value):
    return lax.ppermute(value, "groups", [(0, 1), (1, 0)])


def after(values, others):
    return lax.optimization_barrier((values, others))[0]


def gathered(block):
    first = lax.axis_index("groups") == 0
    below, above = UP(block), DOWN(block)
    two = UP(below)
    beside = [
        ACROSS(jnp.where(first, block, above)),
        ACROSS(jnp.where(first, below, two)),
    ]
    passed = [other_group(value) for value in beside]
    mine = [block, above, two, below, beside[0], passed[0], beside[1], passed[1]]
    return mine, (below, above), beside[1]


def place(me, d_core, d_y, d_z):
    z, y, core = me // 4, (me // 2) % 2, me % 2
    y, core = y + d_y - 2 * y * d_y, core + d_core - 2 * core * d_core
    return ((z + d_z) % 4) * 4 + y * 2 + core


def piece_order():
    me, group = lax.axis_index("ctx"), lax.axis_index("groups")
    order = []
    for d_core in range(2):
        order += [place(me, d_core, 0, d_z) for d_z in range(4)]
        order += [
            place(me, d_core, 1, d_z) for d_z in (group, 1 - group, 3 - group, 2 + group)
        ]
    return jnp.stack(order).astype(jnp.int32)


def relative_order():
    me = lax.axis_index("ctx")
    order = [place(me, c, y, z) for c in range(2) for y in range(2) for z in range(4)]
    return jnp.stack(order).astype(jnp.int32)


def unpack(total, narrow, model):
    rows, slim = total.shape[0] * 3 // 4, total.shape[0] * 3 // 16
    full = total.shape[1]
    rest = model - full
    tail = total[rows + slim :]
    tail = jnp.concatenate([tail[:, j * rest : (j + 1) * rest] for j in range(slim // 8)], axis=0)
    point = jnp.concatenate([total[rows : rows + slim], tail], axis=1)
    return total[:rows].reshape(rows, 3, narrow), point


def scattered(own_far, own_near, sent_far, sent_near):
    got_far = CORE(sent_far)
    got_near = CORE(sent_near)

    def across(z):
        return ACROSS((own_far[z] + got_far[z].astype(F32)).astype(BF16))

    order = {z: across(z) for z in (2, 1, 3, 0)}

    def held(z):
        return own_near[z] + got_near[z].astype(F32) + order[z].astype(F32)

    two = UP(held(2).astype(BF16))
    one = UP((held(1) + two.astype(F32)).astype(BF16))
    three = DOWN(held(3).astype(BF16))
    return held(0) + one.astype(F32) + three.astype(F32)


def body(
    count,
    tokens,
    dilated_weight,
    pointwise_weight,
    query_key_value_weight,
    slopes,
    chain_labels,
    attention_cotangent,
):
    rows, model = tokens.shape
    taps, narrow = dilated_weight.shape[1:]
    wide = taps * narrow
    columns = query_key_value_weight.shape[1]
    shard = model // PIECES
    slim = narrow // PIECES
    quick = count == PIECES

    flat = dilated_weight.reshape(dilated_weight.shape[0], wide)

    def packed(conv, point):
        point = jnp.concatenate(
            [point[:, j * narrow : (j + 1) * narrow] for j in range(model // narrow)], axis=0
        )
        return jnp.concatenate([conv, point], axis=1)

    if quick:
        mine, step, _ = gathered(flat)
        conv_pieces = mine + [CORE(value) for value in mine]
        rest = after(packed(query_key_value_weight, pointwise_weight), step)
        rest_mine, _, late = gathered(rest)
        cotangent = after(attention_cotangent, late)
        index, relative = piece_order(), relative_order()
    else:
        all_flat = lax.all_gather(flat, "ctx", axis=0, tiled=True)
        all_point = lax.all_gather(pointwise_weight, "ctx", axis=0, tiled=True)
        all_projection = lax.all_gather(query_key_value_weight, "ctx", axis=0, tiled=True)
        conv_pieces = [all_flat[i * shard : (i + 1) * shard] for i in range(PIECES)]
        rest_pieces = [
            packed(
                all_projection[i * shard : (i + 1) * shard], all_point[i * slim : (i + 1) * slim]
            )
            for i in range(PIECES)
        ]
        index = relative = jnp.arange(PIECES, dtype=jnp.int32)
        cotangent = attention_cotangent

    from_before = neighbours(tokens[rows - DILATION_STEP :], count)[0]
    from_after = neighbours(tokens[:DILATION_STEP], count)[1]
    span = rows + 2 * DILATION_STEP
    extended, tokens_own, tokens_sent = pl.pallas_call(
        extend_kernel,
        out_shape=(jax.ShapeDtypeStruct((span, model), BF16),)
        + (jax.ShapeDtypeStruct((model // 2, span), BF16),) * 2,
        in_specs=[SMEM] + [VMEM] * 3,
        out_specs=(VMEM,) * 3,
        scratch_shapes=[pltpu.VMEM((model, span), BF16)],
        compiler_params=params(14),
        name="extend",
    )(relative, from_before, tokens, from_after)

    start = lax.axis_index("ctx") * rows
    chain_pad = jnp.pad(chain_labels, (rows, rows), constant_values=-1)
    near_chain = lax.dynamic_slice_in_dim(chain_pad, start, 3 * rows)
    chain_rows = [near_chain[i * rows : (i + 1) * rows].reshape(1, rows) for i in range(3)]
    chain_column = near_chain[rows : 2 * rows].reshape(rows, 1)

    def bf16(*shape):
        return jax.ShapeDtypeStruct(shape, BF16)

    def f32(*shape):
        return jax.ShapeDtypeStruct(shape, F32)

    pre, hidden = pl.pallas_call(
        conv_kernel,
        out_shape=(f32(rows, narrow), bf16(rows, narrow)),
        in_specs=[SMEM, VMEM] + [HBM] * PIECES,
        out_specs=(VMEM, VMEM),
        scratch_shapes=[
            pltpu.VMEM((model, wide), BF16),
            pltpu.SemaphoreType.DMA((PIECES,)),
        ],
        compiler_params=params(14),
        name="conv",
    )(index, extended, *[in_hbm(piece) for piece in conv_pieces])

    if quick:
        last, hidden = lax.optimization_barrier((rest_mine[LATE:], hidden))
        rest_mine = rest_mine[:LATE] + last
        rest_pieces = rest_mine + [CORE(value) for value in rest_mine]
    mixed, inv, query, kv, projection, point = pl.pallas_call(
        project_kernel,
        out_shape=(
            f32(rows, model),
            f32(rows, 1),
            bf16(rows, KEY_COLS),
            bf16(rows, columns - KEY_COLS),
            bf16(model, columns),
            bf16(narrow, model),
        ),
        in_specs=[SMEM, VMEM, VMEM] + [HBM] * PIECES,
        out_specs=(VMEM,) * 6,
        scratch_shapes=[
            pltpu.VMEM((PIECES, shard, narrow), BF16),
            pltpu.VMEM((narrow, model), F32),
            pltpu.SemaphoreType.DMA((2, PIECES)),
        ],
        compiler_params=params(24),
        name="project",
    )(index, extended, hidden, *[in_hbm(piece) for piece in rest_pieces])

    d_prev, d_next = neighbours(cotangent, count)
    kv, d_prev, d_next = lax.optimization_barrier((kv, d_prev, d_next))
    kv_prev, kv_next = neighbours(kv, count)
    q_prev, q_next = neighbours(query, count)

    attended, d_query, stats = pl.pallas_call(
        attend_kernel,
        out_shape=(bf16(rows, HEADS * VAL), bf16(rows, KEY_COLS), f32(2 * HEADS, rows)),
        in_specs=[SMEM, VMEM, HBM, VMEM, HBM] + [VMEM] * 5,
        out_specs=(VMEM,) * 3,
        scratch_shapes=[
            pltpu.VMEM(kv.shape, BF16),
            pltpu.VMEM(kv.shape, BF16),
            pltpu.SemaphoreType.DMA((2,)),
        ],
        compiler_params=params(20),
        name="attend",
    )(
        slopes,
        query,
        in_hbm(kv_prev),
        kv,
        in_hbm(kv_next),
        attention_cotangent,
        chain_column,
        *chain_rows,
    )

    s_prev, s_next = neighbours(stats, count)

    def key_grad(shifts, groups, more, kind, name):
        return pl.pallas_call(
            functools.partial(key_grad_kernel, shifts),
            out_shape=jax.ShapeDtypeStruct(kv.shape, kind),
            in_specs=[SMEM] + [VMEM] * (2 + 4 * len(groups) + len(more)),
            out_specs=VMEM,
            compiler_params=params(14),
            name=name,
        )(slopes, kv, chain_column, *[ref for group in groups for ref in group], *more)

    own = key_grad(
        (0,), [(query, attention_cotangent, stats, chain_rows[1])], [], F32, "own_key_grad"
    )
    d_kv = key_grad(
        (1, -1),
        [(q_prev, d_prev, s_prev, chain_rows[0]), (q_next, d_next, s_next, chain_rows[2])],
        [own],
        BF16,
        "key_grad",
    )

    tail = slim * 4 // 3
    d_mixed, point_own, point_sent = pl.pallas_call(
        mix_back_kernel,
        out_shape=(bf16(rows, model),) + (f32(8, tail, wide),) * 2,
        in_specs=[SMEM] + [VMEM] * 6,
        out_specs=(VMEM,) * 3,
        scratch_shapes=[pltpu.VMEM((narrow, model), F32)],
        compiler_params=params(20),
        name="mix_back",
    )(relative, d_query, d_kv, projection, mixed, inv, hidden)

    own_shapes, sent_shapes = (
        (jax.ShapeDtypeStruct((4, shard + tail, wide), kind),) * 2
        for kind in (F32, BF16 if quick else F32)
    )
    shifted, *sent = pl.pallas_call(
        conv_back_kernel,
        out_shape=(bf16(span, wide),) + sent_shapes,
        in_specs=[VMEM] * 5,
        out_specs=(VMEM,) * 3,
        compiler_params=params(20),
        name="conv_back",
    )(d_mixed, point, pre, tokens_sent, point_sent)
    own = pl.pallas_call(
        conv_own_kernel,
        out_shape=own_shapes,
        in_specs=[VMEM] * 3,
        out_specs=(VMEM,) * 2,
        compiler_params=params(20),
        name="conv_own",
    )(shifted, tokens_own, point_own)

    if quick:
        total = scattered(own[1], own[0], sent[1], sent[0])
        dilated_grad, point_grad = unpack(total, narrow, model)
    else:
        parts = [
            unpack(block[i], narrow, model) for block in (*own, *sent) for i in range(4)
        ]
        dilated_grad, point_grad = (
            lax.psum_scatter(
                jnp.concatenate([part[k] for part in parts], axis=0),
                "ctx",
                scatter_dimension=0,
                tiled=True,
            )
            for k in range(2)
        )
    return (attended, dilated_grad, point_grad)


def solution(mesh):
    return jax.shard_map(
        functools.partial(body, mesh.shape["ctx"]),
        mesh=mesh,
        in_specs=(
            P(("groups", "ctx"), None),
            P("ctx", None, None),
            P("ctx", None),
            P("ctx", None),
            P(),
            P("groups"),
            P(("groups", "ctx"), None),
        ),
        out_specs=(
            P(("groups", "ctx"), None),
            P(("groups", "ctx"), None, None),
            P(("groups", "ctx"), None),
        ),
        check_vma=False,
    )
```

```python
import functools
import math

import jax
import jax.numpy as jnp
from jax import lax
from jax.experimental import pallas as pl
from jax.experimental.pallas import tpu as pltpu
from jax.sharding import PartitionSpec as P

HEADS = 4
KEY = 64
VAL = 192
DILATION_STEP = 16
KEY_COLS = HEADS * KEY
FAR = 1e33
SCALE = 1.0 / math.sqrt(KEY)
GELU_C = math.sqrt(2.0 / math.pi)
PIECES = 16

F32 = jnp.float32
BF16 = jnp.bfloat16
VMEM = pl.BlockSpec(memory_space=pltpu.VMEM)
SMEM = pl.BlockSpec(memory_space=pltpu.SMEM)
HBM = pl.BlockSpec(memory_space=pltpu.HBM)


def dot(a, b):
    return jnp.dot(a, b, preferred_element_type=F32)


def dot_t(a, b):
    return lax.dot_general(a, b, (((1,), (1,)), ((), ())), preferred_element_type=F32)


def in_hbm(value):
    return pltpu.with_memory_space_constraint(value, pltpu.HBM)


def params(mib):
    return pltpu.CompilerParams(vmem_limit_bytes=mib << 20)


def extend(before, tokens, after, extended):
    step, rows = before.shape[0], tokens.shape[0]
    extended[:step, :] = before[...]
    extended[step : step + rows, :] = tokens[...]
    extended[step + rows :, :] = after[...]


def turn_kernel(order, before, tokens, after, own_out, sent_out, extended, turned, halves, sems):
    extend(before, tokens, after, extended)
    turned[...] = extended[...].astype(F32).T.astype(BF16)
    shard = turned.shape[0] // PIECES
    copies = []
    for half, out in enumerate((own_out, sent_out)):
        for k in range(8):
            start = pl.multiple_of(order[8 * half + k] * shard, shard)
            halves[half, k * shard : (k + 1) * shard, :] = turned[pl.ds(start, shard), :]
        copies.append(pltpu.make_async_copy(halves.at[half], out, sems.at[half]))
        copies[-1].start()
    for copy in copies:
        copy.wait()


def front_kernel(index, before, tokens, after, *refs):
    conv, rest = refs[:PIECES], refs[PIECES : 2 * PIECES]
    query, kv, *outs = refs[2 * PIECES : 2 * PIECES + 7]
    pre, hidden, mixed, projection, point, weight, extended, blocks, wide, ins, sems = refs[
        2 * PIECES + 7 :
    ]
    written = []

    def write(ref, number):
        copy = pltpu.make_async_copy(ref, outs[number], sems.at[number])
        copy.start()
        written.append(copy)

    rows = rest[0].shape[0]
    columns = projection.shape[1]
    arriving = []
    for i in range(PIECES):
        here = pl.ds(pl.multiple_of(index[i] * rows, rows), rows)
        arriving.append(
            (
                pltpu.make_async_copy(conv[i], weight.at[:, here], ins.at[0, i]),
                pltpu.make_async_copy(rest[i].at[:, columns:], blocks.at[i], ins.at[1, i]),
                pltpu.make_async_copy(rest[i].at[:, :columns], projection.at[here], ins.at[2, i]),
            )
        )
    for kind in range(3):
        for copies in arriving:
            copies[kind].start()
    extend(before, tokens, after, extended)
    for copies in arriving:
        copies[0].wait()
    count = pre.shape[0]
    total = None
    for tap in range(3):
        shift = tap * DILATION_STEP
        part = dot(extended[shift : shift + count, :], weight[tap])
        total = part if total is None else total + part
    pre[...] = total
    write(pre, 0)
    inner = jnp.tanh(GELU_C * (total + 0.044715 * (total * total * total)))
    hidden[...] = (total * (0.5 * (1.0 + inner))).astype(BF16)
    write(hidden, 1)
    for copies in arriving:
        copies[1].wait()
    slim = rows // 4
    width = blocks.shape[2]
    for i in range(PIECES):
        block = blocks[i].astype(F32)
        here = pl.ds(pl.multiple_of(index[i] * slim, 8), slim)
        for j in range(4):
            wide[here, j * width : (j + 1) * width] = block[j * slim : (j + 1) * slim]
    point[...] = wide[...].astype(BF16)
    write(point, 4)
    mix = tokens[...].astype(F32) + dot(hidden[...], point[...])
    mixed[...] = mix
    write(mixed, 2)
    scale = lax.rsqrt(jnp.mean(mix * mix, axis=1, keepdims=True) + 1e-06)
    normed = (mix * scale).astype(BF16)
    for copies in arriving:
        copies[2].wait()
    write(projection, 3)
    kv[...] = dot(normed, projection[:, KEY_COLS:]).astype(BF16)
    query[...] = dot(normed, projection[:, :KEY_COLS]).astype(BF16)
    for copy in written:
        copy.wait()


def distance(shape, shift):
    a = lax.broadcasted_iota(jnp.int32, shape, 0)
    b = lax.broadcasted_iota(jnp.int32, shape, 1)
    return jnp.abs(a - b + shift).astype(F32)


def masked_distance(same, shift):
    return jnp.where(same, distance(same.shape, shift), FAR)


def attend_kernel(
    slopes, query, kv_prev, kv, kv_next, d_out, q_chain, k_prev, k_own, k_next, *refs
):
    attended, d_query, stats, before, after, sems = refs
    copies = [
        pltpu.make_async_copy(kv_prev, before, sems.at[0]),
        pltpu.make_async_copy(kv_next, after, sems.at[1]),
    ]
    for copy in copies:
        copy.start()
    count = query.shape[0]
    near = (before, kv, after)
    away = [
        masked_distance(q_chain[...] == chain[...], shift)
        for chain, shift in ((k_prev, count), (k_own, 0), (k_next, -count))
    ]
    for copy in copies:
        copy.wait()
    tops, deltas = [], []
    for head in range(HEADS):
        kcols = slice(head * KEY, (head + 1) * KEY)
        vcols = slice(KEY_COLS + head * VAL, KEY_COLS + (head + 1) * VAL)
        ocols = slice(head * VAL, (head + 1) * VAL)
        q = query[:, kcols] * SCALE
        slope = slopes[head]
        scores = [dot_t(q, near[i][:, kcols]) - slope * away[i] for i in range(3)]
        top = jnp.max(
            functools.reduce(jnp.maximum, scores), axis=1, keepdims=True
        )
        expo = [jnp.exp(s - top) for s in scores]
        denom = jnp.sum(expo[0] + expo[1] + expo[2], axis=1, keepdims=True)
        share = 1.0 / denom
        prob = [e * share for e in expo]
        out = sum(dot(p.astype(BF16), near[i][:, vcols]) for i, p in enumerate(prob))
        attended[:, ocols] = out.astype(BF16)
        d_head = d_out[:, ocols]
        delta = jnp.sum(d_head.astype(F32) * out, axis=1, keepdims=True)
        d_q = None
        for i in range(3):
            d_prob = dot_t(d_head, near[i][:, vcols])
            d_score = (prob[i] * (d_prob - delta)).astype(BF16)
            part = dot(d_score, near[i][:, kcols])
            d_q = part if d_q is None else d_q + part
        d_query[:, kcols] = (d_q * SCALE).astype(BF16)
        tops.append(top + jnp.log(denom))
        deltas.append(delta)
    pad = jnp.zeros((count, 128 - 2 * HEADS), F32)
    packed = jnp.concatenate(tops + deltas + [pad], axis=1)
    stats[...] = packed.T[: 2 * HEADS]


def key_grad_kernel(shifts, slopes, kv, k_chain, *refs):
    groups = [refs[4 * i : 4 * i + 4] for i in range(len(shifts))]
    more, d_kv = refs[4 * len(shifts) : -1], refs[-1]
    count = kv.shape[0]
    away = [
        masked_distance(k_chain[...] == group[3][...], shift * count)
        for group, shift in zip(groups, shifts)
    ]
    for head in range(HEADS):
        kcols = slice(head * KEY, (head + 1) * KEY)
        vcols = slice(KEY_COLS + head * VAL, KEY_COLS + (head + 1) * VAL)
        ocols = slice(head * VAL, (head + 1) * VAL)
        k, v, slope = kv[:, kcols] * SCALE, kv[:, vcols], slopes[head]
        d_k = d_v = None
        for i, (query, d_out, stats, _) in enumerate(groups):
            q, d_head = query[:, kcols], d_out[:, ocols]
            score = dot_t(k, q) - slope * away[i]
            back = jnp.exp(score - stats[head : head + 1, :])
            d_prob = dot_t(v, d_head)
            d_score = back * (d_prob - stats[HEADS + head : HEADS + head + 1, :])
            part_k, part_v = dot(d_score.astype(BF16), q), dot(back.astype(BF16), d_head)
            d_k = part_k if d_k is None else d_k + part_k
            d_v = part_v if d_v is None else d_v + part_v
        d_k = d_k * SCALE
        if more:
            d_k, d_v = d_k + more[0][:, kcols], d_v + more[0][:, vcols]
        d_kv[:, kcols] = d_k.astype(d_kv.dtype)
        d_kv[:, vcols] = d_v.astype(d_kv.dtype)


def mix_back_kernel(index, d_query, d_kv, projection, mixed, hidden, d_mixed, *refs):
    *outs, d_point = refs
    d_normed = dot_t(d_query[...], projection[:, :KEY_COLS]) + dot_t(
        d_kv[...], projection[:, KEY_COLS:]
    )
    mix = mixed[...]
    scale = lax.rsqrt(jnp.mean(mix * mix, axis=1, keepdims=True) + 1e-06)
    pull = jnp.mean(d_normed * mix, axis=1, keepdims=True)
    grad = (scale * d_normed - mix * (scale * scale * scale) * pull).astype(BF16)
    d_mixed[...] = grad
    d_point[...] = lax.dot_general(
        hidden[...], grad, (((0,), (0,)), ((), ())), preferred_element_type=F32
    )
    slim = d_point.shape[0] // PIECES
    width = outs[0].shape[2]
    for number in range(PIECES):
        out, k = outs[number // 8], number % 8
        here = pl.ds(pl.multiple_of(index[number] * slim, 8), slim)
        for j in range(d_point.shape[1] // width):
            out[k, j * slim : (j + 1) * slim, :] = d_point[here, j * width : (j + 1) * width]


def put(value, point, outs):
    rows, width = value.shape[0] // 8, point.shape[2]
    for i, out in enumerate(outs):
        for k in range(out.shape[0]):
            number = i * out.shape[0] + k
            for tap in range(3):
                out[k, tap * rows : (tap + 1) * rows, :] = value[
                    number * rows : (number + 1) * rows, tap * width : (tap + 1) * width
                ].astype(out.dtype)
            out[k, 3 * rows :, :] = point[number].astype(out.dtype)


def conv_back_kernel(d_mixed, point, pre, tokens_t, d_point, shifted, *outs):
    count, narrow = pre.shape
    d_hidden = dot_t(d_mixed[...], point[...])
    x = pre[...]
    inner = jnp.tanh(GELU_C * (x + 0.044715 * (x * x * x)))
    slope = 0.5 * (1.0 + inner) + 0.5 * x * (1.0 - inner * inner) * (
        GELU_C * (1.0 + (3 * 0.044715) * (x * x))
    )
    d_pre = (d_hidden * slope).astype(BF16)
    shifted[...] = jnp.zeros_like(shifted)
    for tap in range(3):
        shifted[
            tap * DILATION_STEP : tap * DILATION_STEP + count, tap * narrow : (tap + 1) * narrow
        ] = d_pre
    put(dot(tokens_t[...], shifted[...]), d_point, outs)


def conv_own_kernel(shifted, tokens_t, d_point, *outs):
    put(dot(tokens_t[...], shifted[...]), d_point, outs)


def neighbours(value, count):
    return (
        lax.ppermute(value, "ctx", [(i, i + 1) for i in range(count - 1)]),
        lax.ppermute(value, "ctx", [(i + 1, i) for i in range(count - 1)]),
    )


def ring(step):
    return lambda value: lax.ppermute(
        value, "ctx", [(i, (i + step) % PIECES) for i in range(PIECES)]
    )


def swap(bit):
    return lambda value: lax.ppermute(value, "ctx", [(i, i ^ bit) for i in range(PIECES)])


UP, DOWN, ACROSS, CORE = ring(4), ring(-4), swap(2), swap(1)


def other_group(value):
    return lax.ppermute(value, "groups", [(0, 1), (1, 0)])


def after(values, others):
    return lax.optimization_barrier((values, others))[0]


def gathered(block):
    first = lax.axis_index("groups") == 0
    below, above = UP(block), DOWN(block)
    two = UP(below)
    beside = [ACROSS(jnp.where(first, block, above)), ACROSS(below), ACROSS(two)]
    passed = other_group(beside[0])
    mine = [block, above, two, below, beside[0], passed] + beside[1:]
    return mine, (below, above), beside[2]


def place(me, d_core, d_y, d_z):
    z, y, core = me // 4, (me // 2) % 2, me % 2
    y, core = y + d_y - 2 * y * d_y, core + d_core - 2 * core * d_core
    return ((z + d_z) % 4) * 4 + y * 2 + core


def piece_order():
    me, group = lax.axis_index("ctx"), lax.axis_index("groups")
    order = []
    for d_core in range(2):
        order += [place(me, d_core, 0, d_z) for d_z in range(4)]
        order += [
            place(me, d_core, 1, d_z) for d_z in (group, 1 - group, 3, 2)
        ]
    return jnp.stack(order).astype(jnp.int32)


def relative_order():
    me = lax.axis_index("ctx")
    order = [place(me, c, y, z) for c in range(2) for y in range(2) for z in range(4)]
    return jnp.stack(order).astype(jnp.int32)


def unpack(parts, model):
    width = parts[0].shape[1]
    rows = width // 4
    slim = rows * width // model

    def total(start, count):
        return sum(part[start : start + count].astype(F32) for part in parts)

    conv = total(0, 3 * rows).reshape(3, rows, width).transpose(1, 0, 2)
    blocks = [total(3 * rows + j * slim, slim) for j in range(model // width)]
    return conv, jnp.concatenate(blocks, axis=1)


def scattered(own_far, own_near, sent_far, sent_near):
    got_far = CORE(sent_far)
    got_near = CORE(sent_near)

    def across(z):
        return ACROSS((own_far[z] + got_far[z].astype(F32)).astype(BF16))

    order = {z: across(z) for z in (2, 1, 3, 0)}

    def held(z):
        return own_near[z] + got_near[z].astype(F32) + order[z].astype(F32)

    two = UP(held(2).astype(BF16))
    one = UP((held(1) + two.astype(F32)).astype(BF16))
    three = DOWN(held(3).astype(BF16))
    return own_near[0], got_near[0], order[0], one, three


def body(
    count,
    tokens,
    dilated_weight,
    pointwise_weight,
    query_key_value_weight,
    slopes,
    chain_labels,
    attention_cotangent,
):
    rows, model = tokens.shape
    taps, narrow = dilated_weight.shape[1:]
    wide = taps * narrow
    columns = query_key_value_weight.shape[1]
    shard = model // PIECES
    slim = narrow // PIECES
    quick = count == PIECES

    flat = dilated_weight.transpose(1, 0, 2)

    def packed(conv, point):
        point = jnp.concatenate(
            [point[:, j * narrow : (j + 1) * narrow] for j in range(model // narrow)], axis=0
        )
        return jnp.concatenate([conv, point], axis=1)

    if quick:
        mine, step, _ = gathered(flat)
        conv_pieces = mine + [CORE(value) for value in mine]
        rest = after(packed(query_key_value_weight, pointwise_weight), step)
        rest_mine, _, late = gathered(rest)
        cotangent = after(attention_cotangent, late)
        index, relative = piece_order(), relative_order()
    else:
        all_flat = lax.all_gather(flat, "ctx", axis=1, tiled=True)
        all_point = lax.all_gather(pointwise_weight, "ctx", axis=0, tiled=True)
        all_projection = lax.all_gather(query_key_value_weight, "ctx", axis=0, tiled=True)
        conv_pieces = [all_flat[:, i * shard : (i + 1) * shard] for i in range(PIECES)]
        rest_pieces = [
            packed(
                all_projection[i * shard : (i + 1) * shard], all_point[i * slim : (i + 1) * slim]
            )
            for i in range(PIECES)
        ]
        index = relative = jnp.arange(PIECES, dtype=jnp.int32)
        cotangent = attention_cotangent

    from_before = neighbours(tokens[rows - DILATION_STEP :], count)[0]
    from_after = neighbours(tokens[:DILATION_STEP], count)[1]
    span = rows + 2 * DILATION_STEP
    start = lax.axis_index("ctx") * rows
    chain_pad = jnp.pad(chain_labels, (rows, rows), constant_values=-1)
    near_chain = lax.dynamic_slice_in_dim(chain_pad, start, 3 * rows)
    chain_rows = [near_chain[i * rows : (i + 1) * rows].reshape(1, rows) for i in range(3)]
    chain_column = near_chain[rows : 2 * rows].reshape(rows, 1)

    def bf16(*shape):
        return jax.ShapeDtypeStruct(shape, BF16)

    def f32(*shape):
        return jax.ShapeDtypeStruct(shape, F32)

    if quick:
        rest_pieces = rest_mine + [CORE(value) for value in rest_mine]
    results = (
        ((rows, narrow), F32),
        ((rows, narrow), BF16),
        ((rows, model), F32),
        ((model, columns), BF16),
        ((narrow, model), BF16),
    )
    query, kv, pre, hidden, mixed, projection, point = pl.pallas_call(
        front_kernel,
        out_shape=(bf16(rows, KEY_COLS), bf16(rows, columns - KEY_COLS))
        + tuple(pltpu.HBM(*result) for result in results),
        in_specs=[SMEM] + [VMEM] * 3 + [HBM] * (2 * PIECES),
        out_specs=(VMEM,) * 2 + (HBM,) * 5,
        scratch_shapes=[pltpu.VMEM(*result) for result in results]
        + [
            pltpu.VMEM((taps, model, narrow), BF16),
            pltpu.VMEM((span, model), BF16),
            pltpu.VMEM((PIECES, shard, narrow), BF16),
            pltpu.VMEM((narrow, model), F32),
            pltpu.SemaphoreType.DMA((3, PIECES)),
            pltpu.SemaphoreType.DMA((5,)),
        ],
        compiler_params=params(32),
        name="front",
    )(
        index,
        from_before,
        tokens,
        from_after,
        *[in_hbm(piece) for piece in conv_pieces + rest_pieces],
    )

    turning, kv = lax.optimization_barrier((tokens, kv))
    tokens_own, tokens_sent = pl.pallas_call(
        turn_kernel,
        out_shape=(pltpu.HBM((model // 2, span), BF16),) * 2,
        in_specs=[SMEM] + [VMEM] * 3,
        out_specs=(HBM,) * 2,
        scratch_shapes=[
            pltpu.VMEM((span, model), BF16),
            pltpu.VMEM((model, span), BF16),
            pltpu.VMEM((2, model // 2, span), BF16),
            pltpu.SemaphoreType.DMA((2,)),
        ],
        compiler_params=params(14),
        name="turn",
    )(relative, from_before, turning, from_after)

    d_prev, d_next = neighbours(cotangent, count)
    kv, d_prev, d_next = lax.optimization_barrier((kv, d_prev, d_next))
    kv_prev, kv_next = neighbours(kv, count)
    q_prev, q_next = neighbours(query, count)
    kv_prev, tokens_own, tokens_sent = lax.optimization_barrier(
        (kv_prev, tokens_own, tokens_sent)
    )

    attended, d_query, stats = pl.pallas_call(
        attend_kernel,
        out_shape=(bf16(rows, HEADS * VAL), bf16(rows, KEY_COLS), f32(2 * HEADS, rows)),
        in_specs=[SMEM, VMEM, HBM, VMEM, HBM] + [VMEM] * 5,
        out_specs=(VMEM,) * 3,
        scratch_shapes=[
            pltpu.VMEM(kv.shape, BF16),
            pltpu.VMEM(kv.shape, BF16),
            pltpu.SemaphoreType.DMA((2,)),
        ],
        compiler_params=params(20),
        name="attend",
    )(
        slopes,
        query,
        in_hbm(kv_prev),
        kv,
        in_hbm(kv_next),
        attention_cotangent,
        chain_column,
        *chain_rows,
    )

    s_prev, s_next = neighbours(stats, count)

    def key_grad(shifts, groups, more, kind, name):
        return pl.pallas_call(
            functools.partial(key_grad_kernel, shifts),
            out_shape=jax.ShapeDtypeStruct(kv.shape, kind),
            in_specs=[SMEM] + [VMEM] * (2 + 4 * len(groups) + len(more)),
            out_specs=VMEM,
            compiler_params=params(14),
            name=name,
        )(slopes, kv, chain_column, *[ref for group in groups for ref in group], *more)

    own = key_grad(
        (0,), [(query, attention_cotangent, stats, chain_rows[1])], [], F32, "own_key_grad"
    )
    d_kv = key_grad(
        (1, -1),
        [(q_prev, d_prev, s_prev, chain_rows[0]), (q_next, d_next, s_next, chain_rows[2])],
        [own],
        BF16,
        "key_grad",
    )

    d_mixed, point_own, point_sent = pl.pallas_call(
        mix_back_kernel,
        out_shape=(bf16(rows, model),) + (f32(8, shard, narrow),) * 2,
        in_specs=[SMEM] + [VMEM] * 5,
        out_specs=(VMEM,) * 3,
        scratch_shapes=[pltpu.VMEM((narrow, model), F32)],
        compiler_params=params(20),
        name="mix_back",
    )(relative, d_query, d_kv, projection, mixed, hidden)

    own_shapes, sent_shapes = (
        (jax.ShapeDtypeStruct((4, 4 * shard, narrow), kind),) * 2
        for kind in (F32, BF16 if quick else F32)
    )
    shifted, *sent = pl.pallas_call(
        conv_back_kernel,
        out_shape=(bf16(span, wide),) + sent_shapes,
        in_specs=[VMEM] * 5,
        out_specs=(VMEM,) * 3,
        compiler_params=params(20),
        name="conv_back",
    )(d_mixed, point, pre, tokens_sent, point_sent)
    own = pl.pallas_call(
        conv_own_kernel,
        out_shape=own_shapes,
        in_specs=[VMEM] * 3,
        out_specs=(VMEM,) * 2,
        compiler_params=params(20),
        name="conv_own",
    )(shifted, tokens_own, point_own)

    if quick:
        total = scattered(own[1], own[0], sent[1], sent[0])
        dilated_grad, point_grad = unpack(total, model)
    else:
        parts = [
            unpack([block[i]], model) for block in (*own, *sent) for i in range(4)
        ]
        dilated_grad, point_grad = (
            lax.psum_scatter(
                jnp.concatenate([part[k] for part in parts], axis=0),
                "ctx",
                scatter_dimension=0,
                tiled=True,
            )
            for k in range(2)
        )
    return (attended, dilated_grad, point_grad)


def solution(mesh):
    return jax.shard_map(
        functools.partial(body, mesh.shape["ctx"]),
        mesh=mesh,
        in_specs=(
            P(("groups", "ctx"), None),
            P("ctx", None, None),
            P("ctx", None),
            P("ctx", None),
            P(),
            P("groups"),
            P(("groups", "ctx"), None),
        ),
        out_specs=(
            P(("groups", "ctx"), None),
            P(("groups", "ctx"), None, None),
            P(("groups", "ctx"), None),
        ),
        check_vma=False,
    )
```

```python
import functools
import math

import jax
import jax.numpy as jnp
from jax import lax
from jax.experimental import pallas as pl
from jax.experimental.pallas import tpu as pltpu
from jax.sharding import PartitionSpec as P

HEADS = 4
KEY = 64
VAL = 192
DILATION_STEP = 16
KEY_COLS = HEADS * KEY
FAR = 1e33
SCALE = 1.0 / math.sqrt(KEY)
GELU_C = math.sqrt(2.0 / math.pi)
PIECES = 16

F32 = jnp.float32
BF16 = jnp.bfloat16
VMEM = pl.BlockSpec(memory_space=pltpu.VMEM)
SMEM = pl.BlockSpec(memory_space=pltpu.SMEM)
HBM = pl.BlockSpec(memory_space=pltpu.HBM)


def dot(a, b):
    return jnp.dot(a, b, preferred_element_type=F32)


def dot_t(a, b):
    return lax.dot_general(a, b, (((1,), (1,)), ((), ())), preferred_element_type=F32)


def in_hbm(value):
    return pltpu.with_memory_space_constraint(value, pltpu.HBM)


def params(mib):
    return pltpu.CompilerParams(vmem_limit_bytes=mib << 20)


def extend(before, tokens, after, extended):
    step, rows = before.shape[0], tokens.shape[0]
    extended[:step, :] = before[...]
    extended[step : step + rows, :] = tokens[...]
    extended[step + rows :, :] = after[...]


def turn_kernel(order, before, tokens, after, own_out, sent_out, extended, turned, halves, sems):
    extend(before, tokens, after, extended)
    turned[...] = extended[...].astype(F32).T.astype(BF16)
    shard = turned.shape[0] // PIECES
    copies = []
    for half, out in enumerate((own_out, sent_out)):
        for k in range(8):
            start = pl.multiple_of(order[8 * half + k] * shard, shard)
            halves[half, k * shard : (k + 1) * shard, :] = turned[pl.ds(start, shard), :]
        copies.append(pltpu.make_async_copy(halves.at[half], out, sems.at[half]))
        copies[-1].start()
    for copy in copies:
        copy.wait()


def front_kernel(index, before, tokens, after, *refs):
    conv, rest = refs[:PIECES], refs[PIECES : 2 * PIECES]
    query, kv, *outs = refs[2 * PIECES : 2 * PIECES + 7]
    pre, hidden, mixed, projection, point, weight, extended, blocks, wide, ins, sems = refs[
        2 * PIECES + 7 :
    ]
    written = []

    def write(ref, number):
        copy = pltpu.make_async_copy(ref, outs[number], sems.at[number])
        copy.start()
        written.append(copy)

    rows = rest[0].shape[0]
    columns = projection.shape[1]
    arriving = []
    for i in range(PIECES):
        here = pl.ds(pl.multiple_of(index[i] * rows, rows), rows)
        arriving.append(
            (
                pltpu.make_async_copy(conv[i], weight.at[:, here], ins.at[0, i]),
                pltpu.make_async_copy(rest[i].at[:, columns:], blocks.at[i], ins.at[1, i]),
                pltpu.make_async_copy(rest[i].at[:, :columns], projection.at[here], ins.at[2, i]),
            )
        )
    for kind in range(3):
        for copies in arriving:
            copies[kind].start()
    extend(before, tokens, after, extended)
    for copies in arriving:
        copies[0].wait()
    count = pre.shape[0]
    total = None
    for tap in range(3):
        shift = tap * DILATION_STEP
        part = dot(extended[shift : shift + count, :], weight[tap])
        total = part if total is None else total + part
    pre[...] = total
    write(pre, 0)
    inner = jnp.tanh(GELU_C * (total + 0.044715 * (total * total * total)))
    hidden[...] = (total * (0.5 * (1.0 + inner))).astype(BF16)
    write(hidden, 1)
    for copies in arriving:
        copies[1].wait()
    slim = rows // 4
    width = blocks.shape[2]
    for i in range(PIECES):
        block = blocks[i].astype(F32)
        here = pl.ds(pl.multiple_of(index[i] * slim, 8), slim)
        for j in range(4):
            wide[here, j * width : (j + 1) * width] = block[j * slim : (j + 1) * slim]
    point[...] = wide[...].astype(BF16)
    write(point, 4)
    mix = tokens[...].astype(F32) + dot(hidden[...], point[...])
    mixed[...] = mix
    write(mixed, 2)
    scale = lax.rsqrt(jnp.mean(mix * mix, axis=1, keepdims=True) + 1e-06)
    normed = (mix * scale).astype(BF16)
    for copies in arriving:
        copies[2].wait()
    write(projection, 3)
    kv[...] = dot(normed, projection[:, KEY_COLS:]).astype(BF16)
    query[...] = dot(normed, projection[:, :KEY_COLS]).astype(BF16)
    for copy in written:
        copy.wait()


def distance(shape, shift):
    a = lax.broadcasted_iota(jnp.int32, shape, 0)
    b = lax.broadcasted_iota(jnp.int32, shape, 1)
    return jnp.abs(a - b + shift).astype(F32)


def masked_distance(same, shift):
    return jnp.where(same, distance(same.shape, shift), FAR)


def attend_kernel(
    slopes, sides, query, kv_prev, kv, kv_next, d_out, q_chain, k_prev, k_own, k_next, *refs
):
    attended, d_query, stats, before, after, sems = refs
    copies = [
        pltpu.make_async_copy(kv_prev, before, sems.at[0]),
        pltpu.make_async_copy(kv_next, after, sems.at[1]),
    ]
    for copy in copies:
        copy.start()
    count = query.shape[0]
    near = (before, kv, after)
    away = [
        masked_distance(q_chain[...] == chain[...], shift)
        for chain, shift in ((k_prev, sides[0]), (k_own, 0), (k_next, sides[1]))
    ]
    for copy in copies:
        copy.wait()
    tops, deltas = [], []
    for head in range(HEADS):
        kcols = slice(head * KEY, (head + 1) * KEY)
        vcols = slice(KEY_COLS + head * VAL, KEY_COLS + (head + 1) * VAL)
        ocols = slice(head * VAL, (head + 1) * VAL)
        q = query[:, kcols] * SCALE
        slope = slopes[head]
        scores = [dot_t(q, near[i][:, kcols]) - slope * away[i] for i in range(3)]
        top = jnp.max(
            functools.reduce(jnp.maximum, scores), axis=1, keepdims=True
        )
        expo = [jnp.exp(s - top) for s in scores]
        denom = jnp.sum(expo[0] + expo[1] + expo[2], axis=1, keepdims=True)
        share = 1.0 / denom
        prob = [e * share for e in expo]
        out = sum(dot(p.astype(BF16), near[i][:, vcols]) for i, p in enumerate(prob))
        attended[:, ocols] = out.astype(BF16)
        d_head = d_out[:, ocols]
        delta = jnp.sum(d_head.astype(F32) * out, axis=1, keepdims=True)
        d_q = None
        for i in range(3):
            d_prob = dot_t(d_head, near[i][:, vcols])
            d_score = (prob[i] * (d_prob - delta)).astype(BF16)
            part = dot(d_score, near[i][:, kcols])
            d_q = part if d_q is None else d_q + part
        d_query[:, kcols] = (d_q * SCALE).astype(BF16)
        tops.append(top + jnp.log(denom))
        deltas.append(delta)
    pad = jnp.zeros((count, 128 - 2 * HEADS), F32)
    packed = jnp.concatenate(tops + deltas + [pad], axis=1)
    stats[...] = packed.T[: 2 * HEADS]


def key_grad_kernel(near, slopes, sides, kv, k_chain, *refs):
    shifts = (sides[0], sides[1]) if near else (0,)
    groups = [refs[4 * i : 4 * i + 4] for i in range(len(shifts))]
    more, d_kv = refs[4 * len(shifts) : -1], refs[-1]
    count = kv.shape[0]
    away = [
        masked_distance(k_chain[...] == group[3][...], shift)
        for group, shift in zip(groups, shifts)
    ]
    for head in range(HEADS):
        kcols = slice(head * KEY, (head + 1) * KEY)
        vcols = slice(KEY_COLS + head * VAL, KEY_COLS + (head + 1) * VAL)
        ocols = slice(head * VAL, (head + 1) * VAL)
        k, v, slope = kv[:, kcols] * SCALE, kv[:, vcols], slopes[head]
        d_k = d_v = None
        for i, (query, d_out, stats, _) in enumerate(groups):
            q, d_head = query[:, kcols], d_out[:, ocols]
            score = dot_t(k, q) - slope * away[i]
            back = jnp.exp(score - stats[head : head + 1, :])
            d_prob = dot_t(v, d_head)
            d_score = back * (d_prob - stats[HEADS + head : HEADS + head + 1, :])
            part_k, part_v = dot(d_score.astype(BF16), q), dot(back.astype(BF16), d_head)
            d_k = part_k if d_k is None else d_k + part_k
            d_v = part_v if d_v is None else d_v + part_v
        d_k = d_k * SCALE
        if more:
            d_k, d_v = d_k + more[0][:, kcols], d_v + more[0][:, vcols]
        d_kv[:, kcols] = d_k.astype(d_kv.dtype)
        d_kv[:, vcols] = d_v.astype(d_kv.dtype)


def mix_back_kernel(index, d_query, d_kv, projection, mixed, hidden, d_mixed, *refs):
    *outs, d_point = refs
    d_normed = dot_t(d_query[...], projection[:, :KEY_COLS]) + dot_t(
        d_kv[...], projection[:, KEY_COLS:]
    )
    mix = mixed[...]
    scale = lax.rsqrt(jnp.mean(mix * mix, axis=1, keepdims=True) + 1e-06)
    pull = jnp.mean(d_normed * mix, axis=1, keepdims=True)
    grad = (scale * d_normed - mix * (scale * scale * scale) * pull).astype(BF16)
    d_mixed[...] = grad
    d_point[...] = lax.dot_general(
        hidden[...], grad, (((0,), (0,)), ((), ())), preferred_element_type=F32
    )
    slim = d_point.shape[0] // PIECES
    width = outs[0].shape[2]
    for number in range(PIECES):
        out, k = outs[number // 8], number % 8
        here = pl.ds(pl.multiple_of(index[number] * slim, 8), slim)
        for j in range(d_point.shape[1] // width):
            out[k, j * slim : (j + 1) * slim, :] = d_point[here, j * width : (j + 1) * width]


def put(value, point, outs):
    rows, width = value.shape[0] // 8, point.shape[2]
    for i, out in enumerate(outs):
        for k in range(out.shape[0]):
            number = i * out.shape[0] + k
            for tap in range(3):
                out[k, tap * rows : (tap + 1) * rows, :] = value[
                    number * rows : (number + 1) * rows, tap * width : (tap + 1) * width
                ].astype(out.dtype)
            out[k, 3 * rows :, :] = point[number].astype(out.dtype)


def conv_back_kernel(d_mixed, point, pre, tokens_t, d_point, shifted, *outs):
    count, narrow = pre.shape
    d_hidden = dot_t(d_mixed[...], point[...])
    x = pre[...]
    inner = jnp.tanh(GELU_C * (x + 0.044715 * (x * x * x)))
    slope = 0.5 * (1.0 + inner) + 0.5 * x * (1.0 - inner * inner) * (
        GELU_C * (1.0 + (3 * 0.044715) * (x * x))
    )
    d_pre = (d_hidden * slope).astype(BF16)
    shifted[...] = jnp.zeros_like(shifted)
    for tap in range(3):
        shifted[
            tap * DILATION_STEP : tap * DILATION_STEP + count, tap * narrow : (tap + 1) * narrow
        ] = d_pre
    put(dot(tokens_t[...], shifted[...]), d_point, outs)


def conv_own_kernel(shifted, tokens_t, d_point, *outs):
    put(dot(tokens_t[...], shifted[...]), d_point, outs)


def neighbours(value, count, outer=None):
    pairs = [(i, i ^ 1) for i in range(count)]
    links = [(i, i + 1) for i in range(1, count - 1, 2)]
    links += [(i + 1, i) for i in range(1, count - 1, 2)]
    return (
        lax.ppermute(value, "ctx", pairs),
        lax.ppermute(value if outer is None else outer, "ctx", links),
    )


def ring(step):
    return lambda value: lax.ppermute(
        value, "ctx", [(i, (i + step) % PIECES) for i in range(PIECES)]
    )


def swap(bit):
    return lambda value: lax.ppermute(value, "ctx", [(i, i ^ bit) for i in range(PIECES)])


UP, DOWN, ACROSS, CORE = ring(4), ring(-4), swap(2), swap(1)


def other_group(value):
    return lax.ppermute(value, "groups", [(0, 1), (1, 0)])


def after(values, others):
    return lax.optimization_barrier((values, others))[0]


def gathered(block):
    first = lax.axis_index("groups") == 0
    below, above = UP(block), DOWN(block)
    two = UP(below)
    beside = [ACROSS(jnp.where(first, block, above)), ACROSS(below), ACROSS(two)]
    passed = other_group(beside[0])
    mine = [block, above, two, below, beside[0], passed] + beside[1:]
    return mine, (below, above), beside[2]


def place(me, d_core, d_y, d_z):
    z, y, core = me // 4, (me // 2) % 2, me % 2
    y, core = y + d_y - 2 * y * d_y, core + d_core - 2 * core * d_core
    return ((z + d_z) % 4) * 4 + y * 2 + core


def piece_order():
    me, group = lax.axis_index("ctx"), lax.axis_index("groups")
    order = []
    for d_core in range(2):
        order += [place(me, d_core, 0, d_z) for d_z in range(4)]
        order += [
            place(me, d_core, 1, d_z) for d_z in (group, 1 - group, 3, 2)
        ]
    return jnp.stack(order).astype(jnp.int32)


def relative_order():
    me = lax.axis_index("ctx")
    order = [place(me, c, y, z) for c in range(2) for y in range(2) for z in range(4)]
    return jnp.stack(order).astype(jnp.int32)


def unpack(parts, model):
    width = parts[0].shape[1]
    rows = width // 4
    slim = rows * width // model

    def total(start, count):
        return sum(part[start : start + count].astype(F32) for part in parts)

    conv = total(0, 3 * rows).reshape(3, rows, width).transpose(1, 0, 2)
    blocks = [total(3 * rows + j * slim, slim) for j in range(model // width)]
    return conv, jnp.concatenate(blocks, axis=1)


def scattered(own_far, own_near, sent_far, sent_near):
    got_far = CORE(sent_far)
    got_near = CORE(sent_near)

    def far(z, *more):
        return total(own_far[z], got_far[z], *more)

    def near(z, *more):
        return total(own_near[z], got_near[z], *more)

    def total(*parts):
        return sum(part.astype(F32) for part in parts).astype(BF16)

    two_far = UP(far(2))
    three_beside = ACROSS(far(3))
    two_near = UP(near(2))
    one_beside = ACROSS(far(1, two_far))
    three = DOWN(near(3, three_beside))
    beside = ACROSS(far(0))
    one = UP(near(1, two_near, one_beside))
    return own_near[0], got_near[0], beside, one, three


def body(
    count,
    tokens,
    dilated_weight,
    pointwise_weight,
    query_key_value_weight,
    slopes,
    chain_labels,
    attention_cotangent,
):
    rows, model = tokens.shape
    taps, narrow = dilated_weight.shape[1:]
    wide = taps * narrow
    columns = query_key_value_weight.shape[1]
    shard = model // PIECES
    slim = narrow // PIECES
    quick = count == PIECES

    flat = dilated_weight.transpose(1, 0, 2)

    def packed(conv, point):
        point = jnp.concatenate(
            [point[:, j * narrow : (j + 1) * narrow] for j in range(model // narrow)], axis=0
        )
        return jnp.concatenate([conv, point], axis=1)

    if quick:
        mine, step, _ = gathered(flat)
        conv_pieces = mine + [CORE(value) for value in mine]
        rest = after(packed(query_key_value_weight, pointwise_weight), step)
        rest_mine, _, late = gathered(rest)
        cotangent = after(attention_cotangent, late)
        index, relative = piece_order(), relative_order()
    else:
        all_flat = lax.all_gather(flat, "ctx", axis=1, tiled=True)
        all_point = lax.all_gather(pointwise_weight, "ctx", axis=0, tiled=True)
        all_projection = lax.all_gather(query_key_value_weight, "ctx", axis=0, tiled=True)
        conv_pieces = [all_flat[:, i * shard : (i + 1) * shard] for i in range(PIECES)]
        rest_pieces = [
            packed(
                all_projection[i * shard : (i + 1) * shard], all_point[i * slim : (i + 1) * slim]
            )
            for i in range(PIECES)
        ]
        index = relative = jnp.arange(PIECES, dtype=jnp.int32)
        cotangent = attention_cotangent

    even = lax.axis_index("ctx") % 2 == 0
    head, tail = tokens[:DILATION_STEP], tokens[rows - DILATION_STEP :]
    inner, outer = neighbours(
        jnp.where(even, tail, head), count, jnp.where(even, head, tail)
    )
    from_before, from_after = jnp.where(even, outer, inner), jnp.where(even, inner, outer)
    span = rows + 2 * DILATION_STEP
    start = lax.axis_index("ctx") * rows
    side = jnp.where(even, 1, -1)
    sides = jnp.stack([-side * rows, side * rows]).astype(jnp.int32)
    chain_pad = jnp.pad(chain_labels, (rows, rows), constant_values=-1)
    chain_rows = [
        lax.dynamic_slice_in_dim(chain_pad, start + (1 + offset) * rows, rows).reshape(1, rows)
        for offset in (side, 0, -side)
    ]
    chain_column = chain_rows[1].reshape(rows, 1)

    def bf16(*shape):
        return jax.ShapeDtypeStruct(shape, BF16)

    def f32(*shape):
        return jax.ShapeDtypeStruct(shape, F32)

    if quick:
        rest_pieces = rest_mine + [CORE(value) for value in rest_mine]
    results = (
        ((rows, narrow), F32),
        ((rows, narrow), BF16),
        ((rows, model), F32),
        ((model, columns), BF16),
        ((narrow, model), BF16),
    )
    query, kv, pre, hidden, mixed, projection, point = pl.pallas_call(
        front_kernel,
        out_shape=(bf16(rows, KEY_COLS), bf16(rows, columns - KEY_COLS))
        + tuple(pltpu.HBM(*result) for result in results),
        in_specs=[SMEM] + [VMEM] * 3 + [HBM] * (2 * PIECES),
        out_specs=(VMEM,) * 2 + (HBM,) * 5,
        scratch_shapes=[pltpu.VMEM(*result) for result in results]
        + [
            pltpu.VMEM((taps, model, narrow), BF16),
            pltpu.VMEM((span, model), BF16),
            pltpu.VMEM((PIECES, shard, narrow), BF16),
            pltpu.VMEM((narrow, model), F32),
            pltpu.SemaphoreType.DMA((3, PIECES)),
            pltpu.SemaphoreType.DMA((5,)),
        ],
        compiler_params=params(32),
        name="front",
    )(
        index,
        from_before,
        tokens,
        from_after,
        *[in_hbm(piece) for piece in conv_pieces + rest_pieces],
    )

    turning, kv = lax.optimization_barrier((tokens, kv))
    tokens_own, tokens_sent = pl.pallas_call(
        turn_kernel,
        out_shape=(pltpu.HBM((model // 2, span), BF16),) * 2,
        in_specs=[SMEM] + [VMEM] * 3,
        out_specs=(HBM,) * 2,
        scratch_shapes=[
            pltpu.VMEM((span, model), BF16),
            pltpu.VMEM((model, span), BF16),
            pltpu.VMEM((2, model // 2, span), BF16),
            pltpu.SemaphoreType.DMA((2,)),
        ],
        compiler_params=params(14),
        name="turn",
    )(relative, from_before, turning, from_after)

    d_prev, d_next = neighbours(cotangent, count)
    kv, d_prev, d_next = lax.optimization_barrier((kv, d_prev, d_next))
    kv_prev, kv_next = neighbours(kv, count)
    q_prev, q_next = neighbours(query, count)
    kv_prev, tokens_own, tokens_sent = lax.optimization_barrier(
        (kv_prev, tokens_own, tokens_sent)
    )

    attended, d_query, stats = pl.pallas_call(
        attend_kernel,
        out_shape=(bf16(rows, HEADS * VAL), bf16(rows, KEY_COLS), f32(2 * HEADS, rows)),
        in_specs=[SMEM, SMEM, VMEM, HBM, VMEM, HBM] + [VMEM] * 5,
        out_specs=(VMEM,) * 3,
        scratch_shapes=[
            pltpu.VMEM(kv.shape, BF16),
            pltpu.VMEM(kv.shape, BF16),
            pltpu.SemaphoreType.DMA((2,)),
        ],
        compiler_params=params(20),
        name="attend",
    )(
        slopes,
        sides,
        query,
        in_hbm(kv_prev),
        kv,
        in_hbm(kv_next),
        attention_cotangent,
        chain_column,
        *chain_rows,
    )

    s_prev, s_next = neighbours(stats, count)

    def key_grad(near, groups, more, kind, name):
        return pl.pallas_call(
            functools.partial(key_grad_kernel, near),
            out_shape=jax.ShapeDtypeStruct(kv.shape, kind),
            in_specs=[SMEM] * 2 + [VMEM] * (2 + 4 * len(groups) + len(more)),
            out_specs=VMEM,
            compiler_params=params(14),
            name=name,
        )(slopes, sides, kv, chain_column, *[ref for group in groups for ref in group], *more)

    own = key_grad(
        False, [(query, attention_cotangent, stats, chain_rows[1])], [], F32, "own_key_grad"
    )
    d_kv = key_grad(
        True,
        [(q_prev, d_prev, s_prev, chain_rows[0]), (q_next, d_next, s_next, chain_rows[2])],
        [own],
        BF16,
        "key_grad",
    )

    d_mixed, point_own, point_sent = pl.pallas_call(
        mix_back_kernel,
        out_shape=(bf16(rows, model),) + (f32(8, shard, narrow),) * 2,
        in_specs=[SMEM] + [VMEM] * 5,
        out_specs=(VMEM,) * 3,
        scratch_shapes=[pltpu.VMEM((narrow, model), F32)],
        compiler_params=params(20),
        name="mix_back",
    )(relative, d_query, d_kv, projection, mixed, hidden)

    own_shapes, sent_shapes = (
        (jax.ShapeDtypeStruct((4, 4 * shard, narrow), kind),) * 2
        for kind in (F32, BF16 if quick else F32)
    )
    shifted, *sent = pl.pallas_call(
        conv_back_kernel,
        out_shape=(bf16(span, wide),) + sent_shapes,
        in_specs=[VMEM] * 5,
        out_specs=(VMEM,) * 3,
        compiler_params=params(20),
        name="conv_back",
    )(d_mixed, point, pre, tokens_sent, point_sent)
    own = pl.pallas_call(
        conv_own_kernel,
        out_shape=own_shapes,
        in_specs=[VMEM] * 3,
        out_specs=(VMEM,) * 2,
        compiler_params=params(20),
        name="conv_own",
    )(shifted, tokens_own, point_own)

    if quick:
        total = scattered(own[1], own[0], sent[1], sent[0])
        dilated_grad, point_grad = unpack(total, model)
    else:
        parts = [
            unpack([block[i]], model) for block in (*own, *sent) for i in range(4)
        ]
        dilated_grad, point_grad = (
            lax.psum_scatter(
                jnp.concatenate([part[k] for part in parts], axis=0),
                "ctx",
                scatter_dimension=0,
                tiled=True,
            )
            for k in range(2)
        )
    return (attended, dilated_grad, point_grad)


def solution(mesh):
    return jax.shard_map(
        functools.partial(body, mesh.shape["ctx"]),
        mesh=mesh,
        in_specs=(
            P(("groups", "ctx"), None),
            P("ctx", None, None),
            P("ctx", None),
            P("ctx", None),
            P(),
            P("groups"),
            P(("groups", "ctx"), None),
        ),
        out_specs=(
            P(("groups", "ctx"), None),
            P(("groups", "ctx"), None, None),
            P(("groups", "ctx"), None),
        ),
        check_vma=False,
    )
```

```python
import functools
import math

import jax
import jax.numpy as jnp
from jax import lax
from jax.experimental import pallas as pl
from jax.experimental.pallas import tpu as pltpu
from jax.sharding import PartitionSpec as P

HEADS = 4
KEY = 64
VAL = 192
DILATION_STEP = 16
KEY_COLS = HEADS * KEY
FAR = 1e33
SCALE = 1.0 / math.sqrt(KEY)
GELU_C = math.sqrt(2.0 / math.pi)
PIECES = 16

F32 = jnp.float32
BF16 = jnp.bfloat16
VMEM = pl.BlockSpec(memory_space=pltpu.VMEM)
SMEM = pl.BlockSpec(memory_space=pltpu.SMEM)
HBM = pl.BlockSpec(memory_space=pltpu.HBM)


def dot(a, b):
    return jnp.dot(a, b, preferred_element_type=F32)


def dot_t(a, b):
    return lax.dot_general(a, b, (((1,), (1,)), ((), ())), preferred_element_type=F32)


def in_hbm(value):
    return pltpu.with_memory_space_constraint(value, pltpu.HBM)


def params(mib):
    return pltpu.CompilerParams(vmem_limit_bytes=mib << 20)


def extend(before, tokens, after, extended):
    step, rows = before.shape[0], tokens.shape[0]
    extended[:step, :] = before[...]
    extended[step : step + rows, :] = tokens[...]
    extended[step + rows :, :] = after[...]


def turn_kernel(order, before, tokens, after, own_out, sent_out, extended, turned, halves, sems):
    extend(before, tokens, after, extended)
    turned[...] = extended[...].astype(F32).T.astype(BF16)
    shard = turned.shape[0] // PIECES
    copies = []
    for half, out in enumerate((own_out, sent_out)):
        for k in range(8):
            start = pl.multiple_of(order[8 * half + k] * shard, shard)
            halves[half, k * shard : (k + 1) * shard, :] = turned[pl.ds(start, shard), :]
        copies.append(pltpu.make_async_copy(halves.at[half], out, sems.at[half]))
        copies[-1].start()
    for copy in copies:
        copy.wait()


def front_kernel(index, before, tokens, after, *refs):
    conv, rest = refs[:PIECES], refs[PIECES : 2 * PIECES]
    query, kv, *outs = refs[2 * PIECES : 2 * PIECES + 7]
    pre, hidden, mixed, projection, point, weight, extended, blocks, wide, ins, sems = refs[
        2 * PIECES + 7 :
    ]
    written = []

    def write(ref, number):
        copy = pltpu.make_async_copy(ref, outs[number], sems.at[number])
        copy.start()
        written.append(copy)

    rows = rest[0].shape[0]
    columns = projection.shape[1]
    arriving = []
    for i in range(PIECES):
        here = pl.ds(pl.multiple_of(index[i] * rows, rows), rows)
        arriving.append(
            (
                pltpu.make_async_copy(conv[i], weight.at[:, here], ins.at[0, i]),
                pltpu.make_async_copy(rest[i].at[:, columns:], blocks.at[i], ins.at[1, i]),
                pltpu.make_async_copy(rest[i].at[:, :columns], projection.at[here], ins.at[2, i]),
            )
        )
    for kind in range(3):
        for copies in arriving:
            copies[kind].start()
    extend(before, tokens, after, extended)
    for copies in arriving:
        copies[0].wait()
    count = pre.shape[0]
    total = None
    for tap in range(3):
        shift = tap * DILATION_STEP
        part = dot(extended[shift : shift + count, :], weight[tap])
        total = part if total is None else total + part
    pre[...] = total
    write(pre, 0)
    inner = jnp.tanh(GELU_C * (total + 0.044715 * (total * total * total)))
    hidden[...] = (total * (0.5 * (1.0 + inner))).astype(BF16)
    write(hidden, 1)
    for copies in arriving:
        copies[1].wait()
    slim = rows // 4
    width = blocks.shape[2]
    for i in range(PIECES):
        block = blocks[i].astype(F32)
        here = pl.ds(pl.multiple_of(index[i] * slim, 8), slim)
        for j in range(4):
            wide[here, j * width : (j + 1) * width] = block[j * slim : (j + 1) * slim]
    point[...] = wide[...].astype(BF16)
    write(point, 4)
    mix = tokens[...].astype(F32) + dot(hidden[...], point[...])
    mixed[...] = mix
    write(mixed, 2)
    scale = lax.rsqrt(jnp.mean(mix * mix, axis=1, keepdims=True) + 1e-06)
    normed = (mix * scale).astype(BF16)
    for copies in arriving:
        copies[2].wait()
    write(projection, 3)
    kv[...] = dot(normed, projection[:, KEY_COLS:]).astype(BF16)
    query[...] = dot(normed, projection[:, :KEY_COLS]).astype(BF16)
    for copy in written:
        copy.wait()


def distance(shape, shift):
    a = lax.broadcasted_iota(jnp.int32, shape, 0)
    b = lax.broadcasted_iota(jnp.int32, shape, 1)
    return jnp.abs(a - b + shift).astype(F32)


def masked_distance(same, shift):
    return jnp.where(same, distance(same.shape, shift), FAR)


def attend_near_kernel(
    slopes, sides, query, kv_inner, kv, d_out, q_chain, k_inner, k_own, *refs
):
    score_out, inner, sem = refs
    copy = pltpu.make_async_copy(kv_inner, inner, sem)
    copy.start()
    near = (inner, kv)
    away = [
        masked_distance(q_chain[...] == chain[...], shift)
        for chain, shift in ((k_inner, sides[0]), (k_own, 0))
    ]
    copy.wait()
    for head in range(HEADS):
        kcols = slice(head * KEY, (head + 1) * KEY)
        vcols = slice(KEY_COLS + head * VAL, KEY_COLS + (head + 1) * VAL)
        ocols = slice(head * VAL, (head + 1) * VAL)
        q = query[:, kcols] * SCALE
        for i in range(2):
            score_out[2 * head + i] = dot_t(q, near[i][:, kcols]) - slopes[head] * away[i]


def attend_kernel(
    slopes, sides, query, kv_prev, kv, kv_next, d_out, q_chain, k_prev, k_own, k_next, score_out, *refs
):
    attended, d_query, stats, before, after, sems = refs
    copies = [
        pltpu.make_async_copy(kv_prev, before, sems.at[0]),
        pltpu.make_async_copy(kv_next, after, sems.at[1]),
    ]
    for copy in copies:
        copy.start()
    count = query.shape[0]
    near = (before, kv, after)
    away = [
        masked_distance(q_chain[...] == chain[...], shift)
        for chain, shift in ((k_prev, sides[0]), (k_own, 0), (k_next, sides[1]))
    ]
    for copy in copies:
        copy.wait()
    tops, deltas = [], []
    for head in range(HEADS):
        kcols = slice(head * KEY, (head + 1) * KEY)
        vcols = slice(KEY_COLS + head * VAL, KEY_COLS + (head + 1) * VAL)
        ocols = slice(head * VAL, (head + 1) * VAL)
        q = query[:, kcols] * SCALE
        slope = slopes[head]
        scores = [score_out[2 * head], score_out[2 * head + 1]]
        scores.append(dot_t(q, near[2][:, kcols]) - slope * away[2])
        top = jnp.max(
            functools.reduce(jnp.maximum, scores), axis=1, keepdims=True
        )
        expo = [jnp.exp(s - top) for s in scores]
        denom = jnp.sum(expo[0] + expo[1] + expo[2], axis=1, keepdims=True)
        share = 1.0 / denom
        prob = [e * share for e in expo]
        out = sum(dot(p.astype(BF16), near[i][:, vcols]) for i, p in enumerate(prob))
        attended[:, ocols] = out.astype(BF16)
        d_head = d_out[:, ocols]
        delta = jnp.sum(d_head.astype(F32) * out, axis=1, keepdims=True)
        d_q = None
        for i in range(3):
            d_prob = dot_t(d_head, near[i][:, vcols])
            d_score = (prob[i] * (d_prob - delta)).astype(BF16)
            part = dot(d_score, near[i][:, kcols])
            d_q = part if d_q is None else d_q + part
        d_query[:, kcols] = (d_q * SCALE).astype(BF16)
        tops.append(top + jnp.log(denom))
        deltas.append(delta)
    pad = jnp.zeros((count, 128 - 2 * HEADS), F32)
    packed = jnp.concatenate(tops + deltas + [pad], axis=1)
    stats[...] = packed.T[: 2 * HEADS]


def key_grad_kernel(near, slopes, sides, kv, k_chain, *refs):
    shifts = (sides[0], sides[1]) if near else (0,)
    groups = [refs[4 * i : 4 * i + 4] for i in range(len(shifts))]
    more, d_kv = refs[4 * len(shifts) : -1], refs[-1]
    count = kv.shape[0]
    away = [
        masked_distance(k_chain[...] == group[3][...], shift)
        for group, shift in zip(groups, shifts)
    ]
    for head in range(HEADS):
        kcols = slice(head * KEY, (head + 1) * KEY)
        vcols = slice(KEY_COLS + head * VAL, KEY_COLS + (head + 1) * VAL)
        ocols = slice(head * VAL, (head + 1) * VAL)
        k, v, slope = kv[:, kcols] * SCALE, kv[:, vcols], slopes[head]
        d_k = d_v = None
        for i, (query, d_out, stats, _) in enumerate(groups):
            q, d_head = query[:, kcols], d_out[:, ocols]
            score = dot_t(k, q) - slope * away[i]
            back = jnp.exp(score - stats[head : head + 1, :])
            d_prob = dot_t(v, d_head)
            d_score = back * (d_prob - stats[HEADS + head : HEADS + head + 1, :])
            part_k, part_v = dot(d_score.astype(BF16), q), dot(back.astype(BF16), d_head)
            d_k = part_k if d_k is None else d_k + part_k
            d_v = part_v if d_v is None else d_v + part_v
        d_k = d_k * SCALE
        if more:
            d_k, d_v = d_k + more[0][:, kcols], d_v + more[0][:, vcols]
        d_kv[:, kcols] = d_k.astype(d_kv.dtype)
        d_kv[:, vcols] = d_v.astype(d_kv.dtype)


def mix_back_kernel(index, d_query, d_kv, projection, mixed, hidden, d_mixed, *refs):
    *outs, d_point = refs
    d_normed = dot_t(d_query[...], projection[:, :KEY_COLS]) + dot_t(
        d_kv[...], projection[:, KEY_COLS:]
    )
    mix = mixed[...]
    scale = lax.rsqrt(jnp.mean(mix * mix, axis=1, keepdims=True) + 1e-06)
    pull = jnp.mean(d_normed * mix, axis=1, keepdims=True)
    grad = (scale * d_normed - mix * (scale * scale * scale) * pull).astype(BF16)
    d_mixed[...] = grad
    d_point[...] = lax.dot_general(
        hidden[...], grad, (((0,), (0,)), ((), ())), preferred_element_type=F32
    )
    slim = d_point.shape[0] // PIECES
    width = outs[0].shape[2]
    for number in range(PIECES):
        out, k = outs[number // 8], number % 8
        here = pl.ds(pl.multiple_of(index[number] * slim, 8), slim)
        for j in range(d_point.shape[1] // width):
            out[k, j * slim : (j + 1) * slim, :] = d_point[here, j * width : (j + 1) * width]


def put(value, point, outs):
    rows, width = value.shape[0] // 8, point.shape[2]
    for i, out in enumerate(outs):
        for k in range(out.shape[0]):
            number = i * out.shape[0] + k
            for tap in range(3):
                out[k, tap * rows : (tap + 1) * rows, :] = value[
                    number * rows : (number + 1) * rows, tap * width : (tap + 1) * width
                ].astype(out.dtype)
            out[k, 3 * rows :, :] = point[number].astype(out.dtype)


def conv_back_kernel(d_mixed, point, pre, tokens_t, d_point, shifted, *outs):
    count, narrow = pre.shape
    d_hidden = dot_t(d_mixed[...], point[...])
    x = pre[...]
    inner = jnp.tanh(GELU_C * (x + 0.044715 * (x * x * x)))
    slope = 0.5 * (1.0 + inner) + 0.5 * x * (1.0 - inner * inner) * (
        GELU_C * (1.0 + (3 * 0.044715) * (x * x))
    )
    d_pre = (d_hidden * slope).astype(BF16)
    shifted[...] = jnp.zeros_like(shifted)
    for tap in range(3):
        shifted[
            tap * DILATION_STEP : tap * DILATION_STEP + count, tap * narrow : (tap + 1) * narrow
        ] = d_pre
    put(dot(tokens_t[...], shifted[...]), d_point, outs)


def conv_own_kernel(shifted, tokens_t, d_point, *outs):
    put(dot(tokens_t[...], shifted[...]), d_point, outs)


def neighbours(value, count, outer=None):
    pairs = [(i, i ^ 1) for i in range(count)]
    links = [(i, i + 1) for i in range(1, count - 1, 2)]
    links += [(i + 1, i) for i in range(1, count - 1, 2)]
    return (
        lax.ppermute(value, "ctx", pairs),
        lax.ppermute(value if outer is None else outer, "ctx", links),
    )


def ring(step):
    return lambda value: lax.ppermute(
        value, "ctx", [(i, (i + step) % PIECES) for i in range(PIECES)]
    )


def swap(bit):
    return lambda value: lax.ppermute(value, "ctx", [(i, i ^ bit) for i in range(PIECES)])


UP, DOWN, ACROSS, CORE = ring(4), ring(-4), swap(2), swap(1)


def other_group(value):
    return lax.ppermute(value, "groups", [(0, 1), (1, 0)])


def after(values, others):
    return lax.optimization_barrier((values, others))[0]


def gathered(block):
    first = lax.axis_index("groups") == 0
    below, above = UP(block), DOWN(block)
    two = UP(below)
    beside = [ACROSS(jnp.where(first, block, above)), ACROSS(below), ACROSS(two)]
    passed = other_group(beside[0])
    mine = [block, above, two, below, beside[0], passed] + beside[1:]
    return mine, (below, above), beside[2]


def place(me, d_core, d_y, d_z):
    z, y, core = me // 4, (me // 2) % 2, me % 2
    y, core = y + d_y - 2 * y * d_y, core + d_core - 2 * core * d_core
    return ((z + d_z) % 4) * 4 + y * 2 + core


def piece_order():
    me, group = lax.axis_index("ctx"), lax.axis_index("groups")
    order = []
    for d_core in range(2):
        order += [place(me, d_core, 0, d_z) for d_z in range(4)]
        order += [
            place(me, d_core, 1, d_z) for d_z in (group, 1 - group, 3, 2)
        ]
    return jnp.stack(order).astype(jnp.int32)


def relative_order():
    me = lax.axis_index("ctx")
    order = [place(me, c, y, z) for c in range(2) for y in range(2) for z in range(4)]
    return jnp.stack(order).astype(jnp.int32)


def unpack(parts, model):
    width = parts[0].shape[1]
    rows = width // 4
    slim = rows * width // model

    def total(start, count):
        return sum(part[start : start + count].astype(F32) for part in parts)

    conv = total(0, 3 * rows).reshape(3, rows, width).transpose(1, 0, 2)
    blocks = [total(3 * rows + j * slim, slim) for j in range(model // width)]
    return conv, jnp.concatenate(blocks, axis=1)


def scattered(own_far, own_near, sent_far, sent_near):
    got_far = CORE(sent_far)
    got_near = CORE(sent_near)

    def far(z, *more):
        return total(own_far[z], got_far[z], *more)

    def near(z, *more):
        return total(own_near[z], got_near[z], *more)

    def total(*parts):
        return sum(part.astype(F32) for part in parts).astype(BF16)

    two_far = UP(far(2))
    three_beside = ACROSS(far(3))
    two_near = UP(near(2))
    one_beside = ACROSS(far(1, two_far))
    three = DOWN(near(3, three_beside))
    beside = ACROSS(far(0))
    one = UP(near(1, two_near, one_beside))
    return own_near[0], got_near[0], beside, one, three


def body(
    count,
    tokens,
    dilated_weight,
    pointwise_weight,
    query_key_value_weight,
    slopes,
    chain_labels,
    attention_cotangent,
):
    rows, model = tokens.shape
    taps, narrow = dilated_weight.shape[1:]
    wide = taps * narrow
    columns = query_key_value_weight.shape[1]
    shard = model // PIECES
    slim = narrow // PIECES
    quick = count == PIECES

    flat = dilated_weight.transpose(1, 0, 2)

    def packed(conv, point):
        point = jnp.concatenate(
            [point[:, j * narrow : (j + 1) * narrow] for j in range(model // narrow)], axis=0
        )
        return jnp.concatenate([conv, point], axis=1)

    if quick:
        mine, step, _ = gathered(flat)
        conv_pieces = mine + [CORE(value) for value in mine]
        rest = after(packed(query_key_value_weight, pointwise_weight), step)
        rest_mine, _, late = gathered(rest)
        cotangent = after(attention_cotangent, late)
        index, relative = piece_order(), relative_order()
    else:
        all_flat = lax.all_gather(flat, "ctx", axis=1, tiled=True)
        all_point = lax.all_gather(pointwise_weight, "ctx", axis=0, tiled=True)
        all_projection = lax.all_gather(query_key_value_weight, "ctx", axis=0, tiled=True)
        conv_pieces = [all_flat[:, i * shard : (i + 1) * shard] for i in range(PIECES)]
        rest_pieces = [
            packed(
                all_projection[i * shard : (i + 1) * shard], all_point[i * slim : (i + 1) * slim]
            )
            for i in range(PIECES)
        ]
        index = relative = jnp.arange(PIECES, dtype=jnp.int32)
        cotangent = attention_cotangent

    even = lax.axis_index("ctx") % 2 == 0
    head, tail = tokens[:DILATION_STEP], tokens[rows - DILATION_STEP :]
    inner, outer = neighbours(
        jnp.where(even, tail, head), count, jnp.where(even, head, tail)
    )
    from_before, from_after = jnp.where(even, outer, inner), jnp.where(even, inner, outer)
    span = rows + 2 * DILATION_STEP
    start = lax.axis_index("ctx") * rows
    side = jnp.where(even, 1, -1)
    sides = jnp.stack([-side * rows, side * rows]).astype(jnp.int32)
    chain_pad = jnp.pad(chain_labels, (rows, rows), constant_values=-1)
    chain_rows = [
        lax.dynamic_slice_in_dim(chain_pad, start + (1 + offset) * rows, rows).reshape(1, rows)
        for offset in (side, 0, -side)
    ]
    chain_column = chain_rows[1].reshape(rows, 1)

    def bf16(*shape):
        return jax.ShapeDtypeStruct(shape, BF16)

    def f32(*shape):
        return jax.ShapeDtypeStruct(shape, F32)

    if quick:
        rest_pieces = rest_mine + [CORE(value) for value in rest_mine]
    results = (
        ((rows, narrow), F32),
        ((rows, narrow), BF16),
        ((rows, model), F32),
        ((model, columns), BF16),
        ((narrow, model), BF16),
    )
    query, kv, pre, hidden, mixed, projection, point = pl.pallas_call(
        front_kernel,
        out_shape=(bf16(rows, KEY_COLS), bf16(rows, columns - KEY_COLS))
        + tuple(pltpu.HBM(*result) for result in results),
        in_specs=[SMEM] + [VMEM] * 3 + [HBM] * (2 * PIECES),
        out_specs=(VMEM,) * 2 + (HBM,) * 5,
        scratch_shapes=[pltpu.VMEM(*result) for result in results]
        + [
            pltpu.VMEM((taps, model, narrow), BF16),
            pltpu.VMEM((span, model), BF16),
            pltpu.VMEM((PIECES, shard, narrow), BF16),
            pltpu.VMEM((narrow, model), F32),
            pltpu.SemaphoreType.DMA((3, PIECES)),
            pltpu.SemaphoreType.DMA((5,)),
        ],
        compiler_params=params(32),
        name="front",
    )(
        index,
        from_before,
        tokens,
        from_after,
        *[in_hbm(piece) for piece in conv_pieces + rest_pieces],
    )

    turning, kv = lax.optimization_barrier((tokens, kv))
    tokens_own, tokens_sent = pl.pallas_call(
        turn_kernel,
        out_shape=(pltpu.HBM((model // 2, span), BF16),) * 2,
        in_specs=[SMEM] + [VMEM] * 3,
        out_specs=(HBM,) * 2,
        scratch_shapes=[
            pltpu.VMEM((span, model), BF16),
            pltpu.VMEM((model, span), BF16),
            pltpu.VMEM((2, model // 2, span), BF16),
            pltpu.SemaphoreType.DMA((2,)),
        ],
        compiler_params=params(14),
        name="turn",
    )(relative, from_before, turning, from_after)

    d_prev, d_next = neighbours(cotangent, count)
    kv, d_prev, d_next = lax.optimization_barrier((kv, d_prev, d_next))
    kv_prev, kv_next = neighbours(kv, count)
    q_prev, q_next = neighbours(query, count)
    early = pl.pallas_call(
        attend_near_kernel,
        out_shape=(f32(2 * HEADS, rows, rows),) * 1,
        in_specs=[SMEM, SMEM, VMEM, HBM] + [VMEM] * 5,
        out_specs=(VMEM,) * 1,
        scratch_shapes=[pltpu.VMEM(kv.shape, BF16), pltpu.SemaphoreType.DMA(())],
        compiler_params=params(14),
        name="attend_near",
    )(
        slopes,
        sides,
        query,
        in_hbm(kv_prev),
        kv,
        attention_cotangent,
        chain_column,
        chain_rows[0],
        chain_rows[1],
    )
    kv_next, tokens_own, tokens_sent, early = lax.optimization_barrier(
        (kv_next, tokens_own, tokens_sent, early)
    )

    attended, d_query, stats = pl.pallas_call(
        attend_kernel,
        out_shape=(bf16(rows, HEADS * VAL), bf16(rows, KEY_COLS), f32(2 * HEADS, rows)),
        in_specs=[SMEM, SMEM, VMEM, HBM, VMEM, HBM] + [VMEM] * 6,
        out_specs=(VMEM,) * 3,
        scratch_shapes=[
            pltpu.VMEM(kv.shape, BF16),
            pltpu.VMEM(kv.shape, BF16),
            pltpu.SemaphoreType.DMA((2,)),
        ],
        compiler_params=params(20),
        name="attend",
    )(
        slopes,
        sides,
        query,
        in_hbm(kv_prev),
        kv,
        in_hbm(kv_next),
        attention_cotangent,
        chain_column,
        *chain_rows,
        *early,
    )

    s_prev, s_next = neighbours(stats, count)

    def key_grad(near, groups, more, kind, name):
        return pl.pallas_call(
            functools.partial(key_grad_kernel, near),
            out_shape=jax.ShapeDtypeStruct(kv.shape, kind),
            in_specs=[SMEM] * 2 + [VMEM] * (2 + 4 * len(groups) + len(more)),
            out_specs=VMEM,
            compiler_params=params(14),
            name=name,
        )(slopes, sides, kv, chain_column, *[ref for group in groups for ref in group], *more)

    own = key_grad(
        False, [(query, attention_cotangent, stats, chain_rows[1])], [], F32, "own_key_grad"
    )
    d_kv = key_grad(
        True,
        [(q_prev, d_prev, s_prev, chain_rows[0]), (q_next, d_next, s_next, chain_rows[2])],
        [own],
        BF16,
        "key_grad",
    )

    d_mixed, point_own, point_sent = pl.pallas_call(
        mix_back_kernel,
        out_shape=(bf16(rows, model),) + (f32(8, shard, narrow),) * 2,
        in_specs=[SMEM] + [VMEM] * 5,
        out_specs=(VMEM,) * 3,
        scratch_shapes=[pltpu.VMEM((narrow, model), F32)],
        compiler_params=params(20),
        name="mix_back",
    )(relative, d_query, d_kv, projection, mixed, hidden)

    own_shapes, sent_shapes = (
        (jax.ShapeDtypeStruct((4, 4 * shard, narrow), kind),) * 2
        for kind in (F32, BF16 if quick else F32)
    )
    shifted, *sent = pl.pallas_call(
        conv_back_kernel,
        out_shape=(bf16(span, wide),) + sent_shapes,
        in_specs=[VMEM] * 5,
        out_specs=(VMEM,) * 3,
        compiler_params=params(20),
        name="conv_back",
    )(d_mixed, point, pre, tokens_sent, point_sent)
    own = pl.pallas_call(
        conv_own_kernel,
        out_shape=own_shapes,
        in_specs=[VMEM] * 3,
        out_specs=(VMEM,) * 2,
        compiler_params=params(20),
        name="conv_own",
    )(shifted, tokens_own, point_own)

    if quick:
        total = scattered(own[1], own[0], sent[1], sent[0])
        dilated_grad, point_grad = unpack(total, model)
    else:
        parts = [
            unpack([block[i]], model) for block in (*own, *sent) for i in range(4)
        ]
        dilated_grad, point_grad = (
            lax.psum_scatter(
                jnp.concatenate([part[k] for part in parts], axis=0),
                "ctx",
                scatter_dimension=0,
                tiled=True,
            )
            for k in range(2)
        )
    return (attended, dilated_grad, point_grad)


def solution(mesh):
    return jax.shard_map(
        functools.partial(body, mesh.shape["ctx"]),
        mesh=mesh,
        in_specs=(
            P(("groups", "ctx"), None),
            P("ctx", None, None),
            P("ctx", None),
            P("ctx", None),
            P(),
            P("groups"),
            P(("groups", "ctx"), None),
        ),
        out_specs=(
            P(("groups", "ctx"), None),
            P(("groups", "ctx"), None, None),
            P(("groups", "ctx"), None),
        ),
        check_vma=False,
    )
```

```python
import functools
import math

import jax
import jax.numpy as jnp
from jax import lax
from jax.experimental import pallas as pl
from jax.experimental.pallas import tpu as pltpu
from jax.sharding import PartitionSpec as P

HEADS = 4
KEY = 64
VAL = 192
DILATION_STEP = 16
KEY_COLS = HEADS * KEY
FAR = 1e33
SCALE = 1.0 / math.sqrt(KEY)
GELU_C = math.sqrt(2.0 / math.pi)
PIECES = 16

F32 = jnp.float32
BF16 = jnp.bfloat16
VMEM = pl.BlockSpec(memory_space=pltpu.VMEM)
SMEM = pl.BlockSpec(memory_space=pltpu.SMEM)
HBM = pl.BlockSpec(memory_space=pltpu.HBM)


def dot(a, b):
    return jnp.dot(a, b, preferred_element_type=F32)


def dot_t(a, b):
    return lax.dot_general(a, b, (((1,), (1,)), ((), ())), preferred_element_type=F32)


def in_hbm(value):
    return pltpu.with_memory_space_constraint(value, pltpu.HBM)


def params(mib):
    return pltpu.CompilerParams(vmem_limit_bytes=mib << 20)


def extend(before, tokens, after, extended):
    step, rows = before.shape[0], tokens.shape[0]
    extended[:step, :] = before[...]
    extended[step : step + rows, :] = tokens[...]
    extended[step + rows :, :] = after[...]


def turn_kernel(order, before, tokens, after, own_out, sent_out, extended, turned, halves, sems):
    extend(before, tokens, after, extended)
    turned[...] = extended[...].astype(F32).T.astype(BF16)
    shard = turned.shape[0] // PIECES
    copies = []
    for half, out in enumerate((own_out, sent_out)):
        for k in range(8):
            start = pl.multiple_of(order[8 * half + k] * shard, shard)
            halves[half, k * shard : (k + 1) * shard, :] = turned[pl.ds(start, shard), :]
        copies.append(pltpu.make_async_copy(halves.at[half], out, sems.at[half]))
        copies[-1].start()
    for copy in copies:
        copy.wait()


def front_kernel(index, before, tokens, after, *refs):
    conv, rest = refs[:PIECES], refs[PIECES : 2 * PIECES]
    query, kv, *outs = refs[2 * PIECES : 2 * PIECES + 7]
    pre, hidden, mixed, projection, point, weight, extended, blocks, wide, ins, sems = refs[
        2 * PIECES + 7 :
    ]
    written = []

    def write(ref, number):
        copy = pltpu.make_async_copy(ref, outs[number], sems.at[number])
        copy.start()
        written.append(copy)

    rows = rest[0].shape[0]
    columns = projection.shape[1]
    arriving = []
    for i in range(PIECES):
        here = pl.ds(pl.multiple_of(index[i] * rows, rows), rows)
        arriving.append(
            (
                pltpu.make_async_copy(conv[i], weight.at[:, here], ins.at[0, i]),
                pltpu.make_async_copy(rest[i].at[:, columns:], blocks.at[i], ins.at[1, i]),
                pltpu.make_async_copy(rest[i].at[:, :columns], projection.at[here], ins.at[2, i]),
            )
        )
    for kind in range(3):
        for copies in arriving:
            copies[kind].start()
    extend(before, tokens, after, extended)
    for copies in arriving:
        copies[0].wait()
    count = pre.shape[0]
    total = None
    for tap in range(3):
        shift = tap * DILATION_STEP
        part = dot(extended[shift : shift + count, :], weight[tap])
        total = part if total is None else total + part
    for copies in arriving:
        copies[2].wait()
    write(projection, 3)
    pre[...] = total
    write(pre, 0)
    inner = jnp.tanh(GELU_C * (total + 0.044715 * (total * total * total)))
    hidden[...] = (total * (0.5 * (1.0 + inner))).astype(BF16)
    write(hidden, 1)
    for copies in arriving:
        copies[1].wait()
    slim = rows // 4
    width = blocks.shape[2]
    for i in range(PIECES):
        block = blocks[i].astype(F32)
        here = pl.ds(pl.multiple_of(index[i] * slim, 8), slim)
        for j in range(4):
            wide[here, j * width : (j + 1) * width] = block[j * slim : (j + 1) * slim]
    point[...] = wide[...].astype(BF16)
    write(point, 4)
    mix = tokens[...].astype(F32) + dot(hidden[...], point[...])
    mixed[...] = mix
    write(mixed, 2)
    scale = lax.rsqrt(jnp.mean(mix * mix, axis=1, keepdims=True) + 1e-06)
    normed = (mix * scale).astype(BF16)
    kv[...] = dot(normed, projection[:, KEY_COLS:]).astype(BF16)
    query[...] = dot(normed, projection[:, :KEY_COLS]).astype(BF16)
    for copy in written:
        copy.wait()


def distance(shape, shift):
    a = lax.broadcasted_iota(jnp.int32, shape, 0)
    b = lax.broadcasted_iota(jnp.int32, shape, 1)
    return jnp.abs(a - b + shift).astype(F32)


def masked_distance(same, shift):
    return jnp.where(same, distance(same.shape, shift), FAR)


def attend_near_kernel(
    slopes, sides, query, kv_inner, kv, d_out, q_chain, k_inner, k_own, *refs
):
    score_out, inner, sem = refs
    copy = pltpu.make_async_copy(kv_inner, inner, sem)
    copy.start()
    near = (inner, kv)
    away = [
        masked_distance(q_chain[...] == chain[...], shift)
        for chain, shift in ((k_inner, sides[0]), (k_own, 0))
    ]
    copy.wait()
    for head in range(HEADS):
        kcols = slice(head * KEY, (head + 1) * KEY)
        vcols = slice(KEY_COLS + head * VAL, KEY_COLS + (head + 1) * VAL)
        ocols = slice(head * VAL, (head + 1) * VAL)
        q = query[:, kcols] * SCALE
        for i in range(2):
            score_out[2 * head + i] = dot_t(q, near[i][:, kcols]) - slopes[head] * away[i]


def attend_kernel(
    slopes, sides, query, kv_prev, kv, kv_next, d_out, q_chain, k_prev, k_own, k_next, score_out, *refs
):
    attended, d_query, stats, before, after, sems = refs
    copies = [
        pltpu.make_async_copy(kv_prev, before, sems.at[0]),
        pltpu.make_async_copy(kv_next, after, sems.at[1]),
    ]
    for copy in copies:
        copy.start()
    count = query.shape[0]
    near = (before, kv, after)
    away = [
        masked_distance(q_chain[...] == chain[...], shift)
        for chain, shift in ((k_prev, sides[0]), (k_own, 0), (k_next, sides[1]))
    ]
    for copy in copies:
        copy.wait()
    tops, deltas = [], []
    for head in range(HEADS):
        kcols = slice(head * KEY, (head + 1) * KEY)
        vcols = slice(KEY_COLS + head * VAL, KEY_COLS + (head + 1) * VAL)
        ocols = slice(head * VAL, (head + 1) * VAL)
        q = query[:, kcols] * SCALE
        slope = slopes[head]
        scores = [score_out[2 * head], score_out[2 * head + 1]]
        scores.append(dot_t(q, near[2][:, kcols]) - slope * away[2])
        top = jnp.max(
            functools.reduce(jnp.maximum, scores), axis=1, keepdims=True
        )
        expo = [jnp.exp(s - top) for s in scores]
        denom = jnp.sum(expo[0] + expo[1] + expo[2], axis=1, keepdims=True)
        share = 1.0 / denom
        prob = [e * share for e in expo]
        out = sum(dot(p.astype(BF16), near[i][:, vcols]) for i, p in enumerate(prob))
        attended[:, ocols] = out.astype(BF16)
        d_head = d_out[:, ocols]
        delta = jnp.sum(d_head.astype(F32) * out, axis=1, keepdims=True)
        d_q = None
        for i in range(3):
            d_prob = dot_t(d_head, near[i][:, vcols])
            d_score = (prob[i] * (d_prob - delta)).astype(BF16)
            part = dot(d_score, near[i][:, kcols])
            d_q = part if d_q is None else d_q + part
        d_query[:, kcols] = (d_q * SCALE).astype(BF16)
        tops.append(top + jnp.log(denom))
        deltas.append(delta)
    pad = jnp.zeros((count, 128 - 2 * HEADS), F32)
    packed = jnp.concatenate(tops + deltas + [pad], axis=1)
    stats[...] = packed.T[: 2 * HEADS]


def key_grad_kernel(near, slopes, sides, kv, k_chain, *refs):
    shifts = (sides[0], sides[1]) if near else (0,)
    groups = [refs[4 * i : 4 * i + 4] for i in range(len(shifts))]
    more, d_kv = refs[4 * len(shifts) : -1], refs[-1]
    count = kv.shape[0]
    away = [
        masked_distance(k_chain[...] == group[3][...], shift)
        for group, shift in zip(groups, shifts)
    ]
    for head in range(HEADS):
        kcols = slice(head * KEY, (head + 1) * KEY)
        vcols = slice(KEY_COLS + head * VAL, KEY_COLS + (head + 1) * VAL)
        ocols = slice(head * VAL, (head + 1) * VAL)
        k, v, slope = kv[:, kcols] * SCALE, kv[:, vcols], slopes[head]
        d_k = d_v = None
        for i, (query, d_out, stats, _) in enumerate(groups):
            q, d_head = query[:, kcols], d_out[:, ocols]
            score = dot_t(k, q) - slope * away[i]
            back = jnp.exp(score - stats[head : head + 1, :])
            d_prob = dot_t(v, d_head)
            d_score = back * (d_prob - stats[HEADS + head : HEADS + head + 1, :])
            part_k, part_v = dot(d_score.astype(BF16), q), dot(back.astype(BF16), d_head)
            d_k = part_k if d_k is None else d_k + part_k
            d_v = part_v if d_v is None else d_v + part_v
        d_k = d_k * SCALE
        if more:
            d_k, d_v = d_k + more[0][:, kcols], d_v + more[0][:, vcols]
        d_kv[:, kcols] = d_k.astype(d_kv.dtype)
        d_kv[:, vcols] = d_v.astype(d_kv.dtype)


def mix_back_kernel(index, d_query, d_kv, projection, mixed, hidden, d_mixed, *refs):
    *outs, d_point = refs
    d_normed = dot_t(d_query[...], projection[:, :KEY_COLS]) + dot_t(
        d_kv[...], projection[:, KEY_COLS:]
    )
    mix = mixed[...]
    scale = lax.rsqrt(jnp.mean(mix * mix, axis=1, keepdims=True) + 1e-06)
    pull = jnp.mean(d_normed * mix, axis=1, keepdims=True)
    grad = (scale * d_normed - mix * (scale * scale * scale) * pull).astype(BF16)
    d_mixed[...] = grad
    d_point[...] = lax.dot_general(
        hidden[...], grad, (((0,), (0,)), ((), ())), preferred_element_type=F32
    )
    slim = d_point.shape[0] // PIECES
    width = outs[0].shape[2]
    for number in range(PIECES):
        out, k = outs[number // 8], number % 8
        here = pl.ds(pl.multiple_of(index[number] * slim, 8), slim)
        for j in range(d_point.shape[1] // width):
            out[k, j * slim : (j + 1) * slim, :] = d_point[here, j * width : (j + 1) * width]


def put(value, point, outs):
    rows, width = value.shape[0] // 8, point.shape[2]
    for i, out in enumerate(outs):
        for k in range(out.shape[0]):
            number = i * out.shape[0] + k
            for tap in range(3):
                out[k, tap * rows : (tap + 1) * rows, :] = value[
                    number * rows : (number + 1) * rows, tap * width : (tap + 1) * width
                ].astype(out.dtype)
            out[k, 3 * rows :, :] = point[number].astype(out.dtype)


def conv_back_kernel(d_mixed, point, pre, tokens_t, d_point, shifted, *outs):
    count, narrow = pre.shape
    d_hidden = dot_t(d_mixed[...], point[...])
    x = pre[...]
    inner = jnp.tanh(GELU_C * (x + 0.044715 * (x * x * x)))
    slope = 0.5 * (1.0 + inner) + 0.5 * x * (1.0 - inner * inner) * (
        GELU_C * (1.0 + (3 * 0.044715) * (x * x))
    )
    d_pre = (d_hidden * slope).astype(BF16)
    shifted[...] = jnp.zeros_like(shifted)
    for tap in range(3):
        shifted[
            tap * DILATION_STEP : tap * DILATION_STEP + count, tap * narrow : (tap + 1) * narrow
        ] = d_pre
    put(dot(tokens_t[...], shifted[...]), d_point, outs)


def conv_own_kernel(shifted, tokens_t, d_point, *outs):
    put(dot(tokens_t[...], shifted[...]), d_point, outs)


def neighbours(value, count, outer=None):
    pairs = [(i, i ^ 1) for i in range(count)]
    links = [(i, i + 1) for i in range(1, count - 1, 2)]
    links += [(i + 1, i) for i in range(1, count - 1, 2)]
    return (
        lax.ppermute(value, "ctx", pairs),
        lax.ppermute(value if outer is None else outer, "ctx", links),
    )


def ring(step):
    return lambda value: lax.ppermute(
        value, "ctx", [(i, (i + step) % PIECES) for i in range(PIECES)]
    )


def swap(bit):
    return lambda value: lax.ppermute(value, "ctx", [(i, i ^ bit) for i in range(PIECES)])


UP, DOWN, ACROSS, CORE = ring(4), ring(-4), swap(2), swap(1)


def other_group(value):
    return lax.ppermute(value, "groups", [(0, 1), (1, 0)])


def after(values, others):
    return lax.optimization_barrier((values, others))[0]


def gathered(block):
    first = lax.axis_index("groups") == 0
    below, above = UP(block), DOWN(block)
    two = UP(below)
    beside = [ACROSS(jnp.where(first, block, above)), ACROSS(below), ACROSS(two)]
    passed = other_group(beside[0])
    mine = [block, above, two, below, beside[0], passed] + beside[1:]
    return mine, (below, above), beside[2]


def place(me, d_core, d_y, d_z):
    z, y, core = me // 4, (me // 2) % 2, me % 2
    y, core = y + d_y - 2 * y * d_y, core + d_core - 2 * core * d_core
    return ((z + d_z) % 4) * 4 + y * 2 + core


def piece_order():
    me, group = lax.axis_index("ctx"), lax.axis_index("groups")
    order = []
    for d_core in range(2):
        order += [place(me, d_core, 0, d_z) for d_z in range(4)]
        order += [
            place(me, d_core, 1, d_z) for d_z in (group, 1 - group, 3, 2)
        ]
    return jnp.stack(order).astype(jnp.int32)


def relative_order():
    me = lax.axis_index("ctx")
    order = [place(me, c, y, z) for c in range(2) for y in range(2) for z in range(4)]
    return jnp.stack(order).astype(jnp.int32)


def unpack(parts, model):
    width = parts[0].shape[1]
    rows = width // 4
    slim = rows * width // model

    def total(start, count):
        return sum(part[start : start + count].astype(F32) for part in parts)

    conv = total(0, 3 * rows).reshape(3, rows, width).transpose(1, 0, 2)
    blocks = [total(3 * rows + j * slim, slim) for j in range(model // width)]
    return conv, jnp.concatenate(blocks, axis=1)


def scattered(own_far, own_near, sent_far, sent_near):
    got_far = CORE(sent_far)
    got_near = CORE(sent_near)

    def far(z, *more):
        return total(own_far[z], got_far[z], *more)

    def near(z, *more):
        return total(own_near[z], got_near[z], *more)

    def total(*parts):
        return sum(part.astype(F32) for part in parts).astype(BF16)

    two_far = UP(far(2))
    three_beside = ACROSS(far(3))
    two_near = UP(near(2))
    one_beside = ACROSS(far(1, two_far))
    three = DOWN(near(3, three_beside))
    beside = ACROSS(far(0))
    one = UP(near(1, two_near, one_beside))
    return own_near[0], got_near[0], beside, one, three


def body(
    count,
    tokens,
    dilated_weight,
    pointwise_weight,
    query_key_value_weight,
    slopes,
    chain_labels,
    attention_cotangent,
):
    rows, model = tokens.shape
    taps, narrow = dilated_weight.shape[1:]
    wide = taps * narrow
    columns = query_key_value_weight.shape[1]
    shard = model // PIECES
    slim = narrow // PIECES
    quick = count == PIECES

    flat = dilated_weight.transpose(1, 0, 2)

    def packed(conv, point):
        point = jnp.concatenate(
            [point[:, j * narrow : (j + 1) * narrow] for j in range(model // narrow)], axis=0
        )
        return jnp.concatenate([conv, point], axis=1)

    if quick:
        mine, step, _ = gathered(flat)
        conv_pieces = mine + [CORE(value) for value in mine]
        rest = after(packed(query_key_value_weight, pointwise_weight), step)
        rest_mine, _, late = gathered(rest)
        cotangent = after(attention_cotangent, late)
        index, relative = piece_order(), relative_order()
    else:
        all_flat = lax.all_gather(flat, "ctx", axis=1, tiled=True)
        all_point = lax.all_gather(pointwise_weight, "ctx", axis=0, tiled=True)
        all_projection = lax.all_gather(query_key_value_weight, "ctx", axis=0, tiled=True)
        conv_pieces = [all_flat[:, i * shard : (i + 1) * shard] for i in range(PIECES)]
        rest_pieces = [
            packed(
                all_projection[i * shard : (i + 1) * shard], all_point[i * slim : (i + 1) * slim]
            )
            for i in range(PIECES)
        ]
        index = relative = jnp.arange(PIECES, dtype=jnp.int32)
        cotangent = attention_cotangent

    even = lax.axis_index("ctx") % 2 == 0
    head, tail = tokens[:DILATION_STEP], tokens[rows - DILATION_STEP :]
    inner, outer = neighbours(
        jnp.where(even, tail, head), count, jnp.where(even, head, tail)
    )
    from_before, from_after = jnp.where(even, outer, inner), jnp.where(even, inner, outer)
    span = rows + 2 * DILATION_STEP
    start = lax.axis_index("ctx") * rows
    side = jnp.where(even, 1, -1)
    sides = jnp.stack([-side * rows, side * rows]).astype(jnp.int32)
    chain_pad = jnp.pad(chain_labels, (rows, rows), constant_values=-1)
    chain_rows = [
        lax.dynamic_slice_in_dim(chain_pad, start + (1 + offset) * rows, rows).reshape(1, rows)
        for offset in (side, 0, -side)
    ]
    chain_column = chain_rows[1].reshape(rows, 1)

    def bf16(*shape):
        return jax.ShapeDtypeStruct(shape, BF16)

    def f32(*shape):
        return jax.ShapeDtypeStruct(shape, F32)

    if quick:
        rest_pieces = rest_mine + [CORE(value) for value in rest_mine]
    results = (
        ((rows, narrow), F32),
        ((rows, narrow), BF16),
        ((rows, model), F32),
        ((model, columns), BF16),
        ((narrow, model), BF16),
    )
    query, kv, pre, hidden, mixed, projection, point = pl.pallas_call(
        front_kernel,
        out_shape=(bf16(rows, KEY_COLS), bf16(rows, columns - KEY_COLS))
        + tuple(pltpu.HBM(*result) for result in results),
        in_specs=[SMEM] + [VMEM] * 3 + [HBM] * (2 * PIECES),
        out_specs=(VMEM,) * 2 + (HBM,) * 5,
        scratch_shapes=[pltpu.VMEM(*result) for result in results]
        + [
            pltpu.VMEM((taps, model, narrow), BF16),
            pltpu.VMEM((span, model), BF16),
            pltpu.VMEM((PIECES, shard, narrow), BF16),
            pltpu.VMEM((narrow, model), F32),
            pltpu.SemaphoreType.DMA((3, PIECES)),
            pltpu.SemaphoreType.DMA((5,)),
        ],
        compiler_params=params(32),
        name="front",
    )(
        index,
        from_before,
        tokens,
        from_after,
        *[in_hbm(piece) for piece in conv_pieces + rest_pieces],
    )

    turning, kv = lax.optimization_barrier((tokens, kv))
    tokens_own, tokens_sent = pl.pallas_call(
        turn_kernel,
        out_shape=(pltpu.HBM((model // 2, span), BF16),) * 2,
        in_specs=[SMEM] + [VMEM] * 3,
        out_specs=(HBM,) * 2,
        scratch_shapes=[
            pltpu.VMEM((span, model), BF16),
            pltpu.VMEM((model, span), BF16),
            pltpu.VMEM((2, model // 2, span), BF16),
            pltpu.SemaphoreType.DMA((2,)),
        ],
        compiler_params=params(14),
        name="turn",
    )(relative, from_before, turning, from_after)

    d_prev, d_next = neighbours(cotangent, count)
    kv, d_prev, d_next = lax.optimization_barrier((kv, d_prev, d_next))
    kv_prev, kv_next = neighbours(kv, count)
    q_prev, q_next = neighbours(query, count)
    early = pl.pallas_call(
        attend_near_kernel,
        out_shape=(f32(2 * HEADS, rows, rows),) * 1,
        in_specs=[SMEM, SMEM, VMEM, HBM] + [VMEM] * 5,
        out_specs=(VMEM,) * 1,
        scratch_shapes=[pltpu.VMEM(kv.shape, BF16), pltpu.SemaphoreType.DMA(())],
        compiler_params=params(14),
        name="attend_near",
    )(
        slopes,
        sides,
        query,
        in_hbm(kv_prev),
        kv,
        attention_cotangent,
        chain_column,
        chain_rows[0],
        chain_rows[1],
    )
    kv_next, tokens_own, tokens_sent, early = lax.optimization_barrier(
        (kv_next, tokens_own, tokens_sent, early)
    )

    attended, d_query, stats = pl.pallas_call(
        attend_kernel,
        out_shape=(bf16(rows, HEADS * VAL), bf16(rows, KEY_COLS), f32(2 * HEADS, rows)),
        in_specs=[SMEM, SMEM, VMEM, HBM, VMEM, HBM] + [VMEM] * 6,
        out_specs=(VMEM,) * 3,
        scratch_shapes=[
            pltpu.VMEM(kv.shape, BF16),
            pltpu.VMEM(kv.shape, BF16),
            pltpu.SemaphoreType.DMA((2,)),
        ],
        compiler_params=params(20),
        name="attend",
    )(
        slopes,
        sides,
        query,
        in_hbm(kv_prev),
        kv,
        in_hbm(kv_next),
        attention_cotangent,
        chain_column,
        *chain_rows,
        *early,
    )

    s_prev, s_next = neighbours(stats, count)

    def key_grad(near, groups, more, kind, name):
        return pl.pallas_call(
            functools.partial(key_grad_kernel, near),
            out_shape=jax.ShapeDtypeStruct(kv.shape, kind),
            in_specs=[SMEM] * 2 + [VMEM] * (2 + 4 * len(groups) + len(more)),
            out_specs=VMEM,
            compiler_params=params(14),
            name=name,
        )(slopes, sides, kv, chain_column, *[ref for group in groups for ref in group], *more)

    own = key_grad(
        False, [(query, attention_cotangent, stats, chain_rows[1])], [], F32, "own_key_grad"
    )
    d_kv = key_grad(
        True,
        [(q_prev, d_prev, s_prev, chain_rows[0]), (q_next, d_next, s_next, chain_rows[2])],
        [own],
        BF16,
        "key_grad",
    )

    d_mixed, point_own, point_sent = pl.pallas_call(
        mix_back_kernel,
        out_shape=(bf16(rows, model),) + (f32(8, shard, narrow),) * 2,
        in_specs=[SMEM] + [VMEM] * 5,
        out_specs=(VMEM,) * 3,
        scratch_shapes=[pltpu.VMEM((narrow, model), F32)],
        compiler_params=params(20),
        name="mix_back",
    )(relative, d_query, d_kv, projection, mixed, hidden)

    own_shapes, sent_shapes = (
        (jax.ShapeDtypeStruct((4, 4 * shard, narrow), kind),) * 2
        for kind in (F32, BF16 if quick else F32)
    )
    shifted, *sent = pl.pallas_call(
        conv_back_kernel,
        out_shape=(bf16(span, wide),) + sent_shapes,
        in_specs=[VMEM] * 5,
        out_specs=(VMEM,) * 3,
        compiler_params=params(20),
        name="conv_back",
    )(d_mixed, point, pre, tokens_sent, point_sent)
    own = pl.pallas_call(
        conv_own_kernel,
        out_shape=own_shapes,
        in_specs=[VMEM] * 3,
        out_specs=(VMEM,) * 2,
        compiler_params=params(20),
        name="conv_own",
    )(shifted, tokens_own, point_own)

    if quick:
        total = scattered(own[1], own[0], sent[1], sent[0])
        dilated_grad, point_grad = unpack(total, model)
    else:
        parts = [
            unpack([block[i]], model) for block in (*own, *sent) for i in range(4)
        ]
        dilated_grad, point_grad = (
            lax.psum_scatter(
                jnp.concatenate([part[k] for part in parts], axis=0),
                "ctx",
                scatter_dimension=0,
                tiled=True,
            )
            for k in range(2)
        )
    return (attended, dilated_grad, point_grad)


def solution(mesh):
    return jax.shard_map(
        functools.partial(body, mesh.shape["ctx"]),
        mesh=mesh,
        in_specs=(
            P(("groups", "ctx"), None),
            P("ctx", None, None),
            P("ctx", None),
            P("ctx", None),
            P(),
            P("groups"),
            P(("groups", "ctx"), None),
        ),
        out_specs=(
            P(("groups", "ctx"), None),
            P(("groups", "ctx"), None, None),
            P(("groups", "ctx"), None),
        ),
        check_vma=False,
    )
```

```python
import functools
import math

import jax
import jax.numpy as jnp
from jax import lax
from jax.experimental import pallas as pl
from jax.experimental.pallas import tpu as pltpu
from jax.sharding import PartitionSpec as P

HEADS = 4
KEY = 64
VAL = 192
DILATION_STEP = 16
KEY_COLS = HEADS * KEY
FAR = 1e33
SCALE = 1.0 / math.sqrt(KEY)
GELU_C = math.sqrt(2.0 / math.pi)
PIECES = 16

F32 = jnp.float32
BF16 = jnp.bfloat16
VMEM = pl.BlockSpec(memory_space=pltpu.VMEM)
SMEM = pl.BlockSpec(memory_space=pltpu.SMEM)
HBM = pl.BlockSpec(memory_space=pltpu.HBM)


def dot(a, b):
    return jnp.dot(a, b, preferred_element_type=F32)


def dot_t(a, b):
    return lax.dot_general(a, b, (((1,), (1,)), ((), ())), preferred_element_type=F32)


def in_hbm(value):
    return pltpu.with_memory_space_constraint(value, pltpu.HBM)


def params(mib):
    return pltpu.CompilerParams(vmem_limit_bytes=mib << 20)


def extend(before, tokens, after, extended):
    step, rows = before.shape[0], tokens.shape[0]
    extended[:step, :] = before[...]
    extended[step : step + rows, :] = tokens[...]
    extended[step + rows :, :] = after[...]


def turn_kernel(order, before, tokens, after, own_out, sent_out, extended, turned, halves, sems):
    extend(before, tokens, after, extended)
    turned[...] = extended[...].astype(F32).T.astype(BF16)
    shard = turned.shape[0] // PIECES
    copies = []
    for half, out in enumerate((own_out, sent_out)):
        for k in range(8):
            start = pl.multiple_of(order[8 * half + k] * shard, shard)
            halves[half, k * shard : (k + 1) * shard, :] = turned[pl.ds(start, shard), :]
        copies.append(pltpu.make_async_copy(halves.at[half], out, sems.at[half]))
        copies[-1].start()
    for copy in copies:
        copy.wait()


def front_kernel(index, before, tokens, after, *refs):
    conv, rest = refs[:PIECES], refs[PIECES : 2 * PIECES]
    query, kv, *outs = refs[2 * PIECES : 2 * PIECES + 7]
    pre, hidden, mixed, projection, point, weight, extended, blocks, wide, ins, sems = refs[
        2 * PIECES + 7 :
    ]
    written = []

    def write(ref, number):
        copy = pltpu.make_async_copy(ref, outs[number], sems.at[number])
        copy.start()
        written.append(copy)

    rows = rest[0].shape[0]
    columns = projection.shape[1]
    arriving = []
    for i in range(PIECES):
        here = pl.ds(pl.multiple_of(index[i] * rows, rows), rows)
        arriving.append(
            (
                pltpu.make_async_copy(conv[i], weight.at[:, here], ins.at[0, i]),
                pltpu.make_async_copy(rest[i].at[:, columns:], blocks.at[i], ins.at[1, i]),
                pltpu.make_async_copy(rest[i].at[:, :columns], projection.at[here], ins.at[2, i]),
            )
        )
    for kind in range(3):
        for copies in arriving:
            copies[kind].start()
    extend(before, tokens, after, extended)
    for copies in arriving:
        copies[0].wait()
    count = pre.shape[0]
    total = None
    for tap in range(3):
        shift = tap * DILATION_STEP
        part = dot(extended[shift : shift + count, :], weight[tap])
        total = part if total is None else total + part
    for copies in arriving:
        copies[2].wait()
    write(projection, 3)
    pre[...] = total
    write(pre, 0)
    inner = jnp.tanh(GELU_C * (total + 0.044715 * (total * total * total)))
    hidden[...] = (total * (0.5 * (1.0 + inner))).astype(BF16)
    write(hidden, 1)
    for copies in arriving:
        copies[1].wait()
    slim = rows // 4
    width = blocks.shape[2]
    for i in range(PIECES):
        block = blocks[i].astype(F32)
        here = pl.ds(pl.multiple_of(index[i] * slim, 8), slim)
        for j in range(4):
            wide[here, j * width : (j + 1) * width] = block[j * slim : (j + 1) * slim]
    point[...] = wide[...].astype(BF16)
    write(point, 4)
    mix = tokens[...].astype(F32) + dot(hidden[...], point[...])
    mixed[...] = mix
    write(mixed, 2)
    scale = lax.rsqrt(jnp.mean(mix * mix, axis=1, keepdims=True) + 1e-06)
    normed = (mix * scale).astype(BF16)
    kv[...] = dot(normed, projection[:, KEY_COLS:]).astype(BF16)
    query[...] = dot(normed, projection[:, :KEY_COLS]).astype(BF16)
    for copy in written:
        copy.wait()


def distance(shape, shift):
    a = lax.broadcasted_iota(jnp.int32, shape, 0)
    b = lax.broadcasted_iota(jnp.int32, shape, 1)
    return jnp.abs(a - b + shift).astype(F32)


def masked_distance(same, shift):
    return jnp.where(same, distance(same.shape, shift), FAR)


def attend_near_kernel(
    slopes, sides, query, kv_inner, kv, d_out, q_chain, k_inner, k_own, *refs
):
    score_out, inner, sem = refs
    copy = pltpu.make_async_copy(kv_inner, inner, sem)
    copy.start()
    near = (inner, kv)
    away = [
        masked_distance(q_chain[...] == chain[...], shift)
        for chain, shift in ((k_inner, sides[0]), (k_own, 0))
    ]
    copy.wait()
    for head in range(HEADS):
        kcols = slice(head * KEY, (head + 1) * KEY)
        vcols = slice(KEY_COLS + head * VAL, KEY_COLS + (head + 1) * VAL)
        ocols = slice(head * VAL, (head + 1) * VAL)
        q = query[:, kcols] * SCALE
        for i in range(2):
            score_out[2 * head + i] = dot_t(q, near[i][:, kcols]) - slopes[head] * away[i]


def attend_kernel(
    slopes, sides, query, kv_prev, kv, kv_next, d_out, q_chain, k_prev, k_own, k_next, score_out, *refs
):
    attended, d_query, stats, before, after, sems = refs
    copies = [
        pltpu.make_async_copy(kv_prev, before, sems.at[0]),
        pltpu.make_async_copy(kv_next, after, sems.at[1]),
    ]
    for copy in copies:
        copy.start()
    count = query.shape[0]
    near = (before, kv, after)
    away = [
        masked_distance(q_chain[...] == chain[...], shift)
        for chain, shift in ((k_prev, sides[0]), (k_own, 0), (k_next, sides[1]))
    ]
    for copy in copies:
        copy.wait()
    tops, deltas = [], []
    for head in range(HEADS):
        kcols = slice(head * KEY, (head + 1) * KEY)
        vcols = slice(KEY_COLS + head * VAL, KEY_COLS + (head + 1) * VAL)
        ocols = slice(head * VAL, (head + 1) * VAL)
        q = query[:, kcols] * SCALE
        slope = slopes[head]
        scores = [score_out[2 * head], score_out[2 * head + 1]]
        scores.append(dot_t(q, near[2][:, kcols]) - slope * away[2])
        top = jnp.max(
            functools.reduce(jnp.maximum, scores), axis=1, keepdims=True
        )
        expo = [jnp.exp(s - top) for s in scores]
        denom = jnp.sum(expo[0] + expo[1] + expo[2], axis=1, keepdims=True)
        share = 1.0 / denom
        prob = [e * share for e in expo]
        out = sum(dot(p.astype(BF16), near[i][:, vcols]) for i, p in enumerate(prob))
        attended[:, ocols] = out.astype(BF16)
        d_head = d_out[:, ocols]
        delta = jnp.sum(d_head.astype(F32) * out, axis=1, keepdims=True)
        d_q = None
        for i in range(3):
            d_prob = dot_t(d_head, near[i][:, vcols])
            d_score = (prob[i] * (d_prob - delta)).astype(BF16)
            part = dot(d_score, near[i][:, kcols])
            d_q = part if d_q is None else d_q + part
        d_query[:, kcols] = (d_q * SCALE).astype(BF16)
        tops.append(top + jnp.log(denom))
        deltas.append(delta)
    pad = jnp.zeros((count, 128 - 2 * HEADS), F32)
    packed = jnp.concatenate(tops + deltas + [pad], axis=1)
    stats[...] = packed.T[: 2 * HEADS]


def key_grad_kernel(near, slopes, sides, kv, k_chain, *refs):
    shifts = (sides[0], sides[1]) if near else (0,)
    groups = [refs[4 * i : 4 * i + 4] for i in range(len(shifts))]
    more, d_kv = refs[4 * len(shifts) : -1], refs[-1]
    count = kv.shape[0]
    away = [
        masked_distance(k_chain[...] == group[3][...], shift)
        for group, shift in zip(groups, shifts)
    ]
    for head in range(HEADS):
        kcols = slice(head * KEY, (head + 1) * KEY)
        vcols = slice(KEY_COLS + head * VAL, KEY_COLS + (head + 1) * VAL)
        ocols = slice(head * VAL, (head + 1) * VAL)
        k, v, slope = kv[:, kcols] * SCALE, kv[:, vcols], slopes[head]
        d_k = d_v = None
        for i, (query, d_out, stats, _) in enumerate(groups):
            q, d_head = query[:, kcols], d_out[:, ocols]
            score = dot_t(k, q) - slope * away[i]
            back = jnp.exp(score - stats[head : head + 1, :])
            d_prob = dot_t(v, d_head)
            d_score = back * (d_prob - stats[HEADS + head : HEADS + head + 1, :])
            part_k, part_v = dot(d_score.astype(BF16), q), dot(back.astype(BF16), d_head)
            d_k = part_k if d_k is None else d_k + part_k
            d_v = part_v if d_v is None else d_v + part_v
        d_k = d_k * SCALE
        if more:
            d_k, d_v = d_k + more[0][:, kcols], d_v + more[0][:, vcols]
        d_kv[:, kcols] = d_k.astype(d_kv.dtype)
        d_kv[:, vcols] = d_v.astype(d_kv.dtype)


def mix_back_kernel(index, d_query, d_kv, projection, mixed, hidden, d_mixed, *refs):
    *outs, d_point = refs
    d_normed = dot_t(d_query[...], projection[:, :KEY_COLS]) + dot_t(
        d_kv[...], projection[:, KEY_COLS:]
    )
    mix = mixed[...]
    scale = lax.rsqrt(jnp.mean(mix * mix, axis=1, keepdims=True) + 1e-06)
    pull = jnp.mean(d_normed * mix, axis=1, keepdims=True)
    grad = (scale * d_normed - mix * (scale * scale * scale) * pull).astype(BF16)
    d_mixed[...] = grad
    d_point[...] = lax.dot_general(
        hidden[...], grad, (((0,), (0,)), ((), ())), preferred_element_type=F32
    )
    slim = d_point.shape[0] // PIECES
    width = outs[0].shape[2]
    for number in range(PIECES):
        out, k = outs[number // 8], number % 8
        here = pl.ds(pl.multiple_of(index[number] * slim, 8), slim)
        for j in range(d_point.shape[1] // width):
            out[k, j * slim : (j + 1) * slim, :] = d_point[here, j * width : (j + 1) * width]


def put(value, point, outs):
    rows, width = value.shape[0] // 8, point.shape[2]
    for i, out in enumerate(outs):
        for k in range(out.shape[0]):
            number = i * out.shape[0] + k
            for tap in range(3):
                out[k, tap * rows : (tap + 1) * rows, :] = value[
                    number * rows : (number + 1) * rows, tap * width : (tap + 1) * width
                ].astype(out.dtype)
            out[k, 3 * rows :, :] = point[number].astype(out.dtype)


def conv_back_kernel(d_mixed, point, pre, tokens_t, d_point, shifted, *outs):
    count, narrow = pre.shape
    d_hidden = dot_t(d_mixed[...], point[...])
    x = pre[...]
    inner = jnp.tanh(GELU_C * (x + 0.044715 * (x * x * x)))
    slope = 0.5 * (1.0 + inner) + 0.5 * x * (1.0 - inner * inner) * (
        GELU_C * (1.0 + (3 * 0.044715) * (x * x))
    )
    d_pre = (d_hidden * slope).astype(BF16)
    shifted[...] = jnp.zeros_like(shifted)
    for tap in range(3):
        shifted[
            tap * DILATION_STEP : tap * DILATION_STEP + count, tap * narrow : (tap + 1) * narrow
        ] = d_pre
    put(dot(tokens_t[...], shifted[...]), d_point, outs)


def conv_own_kernel(shifted, tokens_t, d_point, *outs):
    put(dot(tokens_t[...], shifted[...]), d_point, outs)


def neighbours(value, count, outer=None):
    pairs = [(i, i ^ 1) for i in range(count)]
    links = [(i, i + 1) for i in range(1, count - 1, 2)]
    links += [(i + 1, i) for i in range(1, count - 1, 2)]
    return (
        lax.ppermute(value, "ctx", pairs),
        lax.ppermute(value if outer is None else outer, "ctx", links),
    )


def ring(step):
    return lambda value: lax.ppermute(
        value, "ctx", [(i, (i + step) % PIECES) for i in range(PIECES)]
    )


def swap(bit):
    return lambda value: lax.ppermute(value, "ctx", [(i, i ^ bit) for i in range(PIECES)])


UP, DOWN, ACROSS, CORE = ring(4), ring(-4), swap(2), swap(1)


def other_group(value):
    return lax.ppermute(value, "groups", [(0, 1), (1, 0)])


def after(values, others):
    return lax.optimization_barrier((values, others))[0]


def gathered(block):
    first = lax.axis_index("groups") == 0
    below, above = UP(block), DOWN(block)
    two = UP(below)
    beside = [ACROSS(jnp.where(first, block, above)), ACROSS(below), ACROSS(two)]
    passed = other_group(beside[0])
    mine = [block, above, two, below, beside[0], passed] + beside[1:]
    return mine, (below, above), beside[2]


def place(me, d_core, d_y, d_z):
    z, y, core = me // 4, (me // 2) % 2, me % 2
    y, core = y + d_y - 2 * y * d_y, core + d_core - 2 * core * d_core
    return ((z + d_z) % 4) * 4 + y * 2 + core


def piece_order():
    me, group = lax.axis_index("ctx"), lax.axis_index("groups")
    order = []
    for d_core in range(2):
        order += [place(me, d_core, 0, d_z) for d_z in range(4)]
        order += [
            place(me, d_core, 1, d_z) for d_z in (group, 1 - group, 3, 2)
        ]
    return jnp.stack(order).astype(jnp.int32)


def relative_order():
    me = lax.axis_index("ctx")
    order = [place(me, c, y, z) for c in range(2) for y in range(2) for z in range(4)]
    return jnp.stack(order).astype(jnp.int32)


def unpack(parts, model):
    width = parts[0].shape[1]
    rows = width // 4
    slim = rows * width // model

    def total(start, count):
        return sum(part[start : start + count].astype(F32) for part in parts)

    conv = total(0, 3 * rows).reshape(3, rows, width).transpose(1, 0, 2)
    blocks = [total(3 * rows + j * slim, slim) for j in range(model // width)]
    return conv, jnp.concatenate(blocks, axis=1)


def scattered(own_far, own_near, sent_far, sent_near):
    got_far = CORE(sent_far)
    got_near = CORE(sent_near)

    def far(z, *more):
        return total(own_far[z], got_far[z], *more)

    def near(z, *more):
        return total(own_near[z], got_near[z], *more)

    def total(*parts):
        return sum(part.astype(F32) for part in parts).astype(BF16)

    two_far = UP(far(2))
    three_beside = ACROSS(far(3))
    one_beside = ACROSS(far(1, two_far))
    two_near = UP(after(near(2), three_beside))
    three = DOWN(near(3, three_beside))
    beside = ACROSS(far(0))
    one = UP(near(1, two_near, one_beside))
    return own_near[0], got_near[0], beside, one, three


def body(
    count,
    tokens,
    dilated_weight,
    pointwise_weight,
    query_key_value_weight,
    slopes,
    chain_labels,
    attention_cotangent,
):
    rows, model = tokens.shape
    taps, narrow = dilated_weight.shape[1:]
    wide = taps * narrow
    columns = query_key_value_weight.shape[1]
    shard = model // PIECES
    slim = narrow // PIECES
    quick = count == PIECES

    flat = dilated_weight.transpose(1, 0, 2)

    def packed(conv, point):
        point = jnp.concatenate(
            [point[:, j * narrow : (j + 1) * narrow] for j in range(model // narrow)], axis=0
        )
        return jnp.concatenate([conv, point], axis=1)

    if quick:
        mine, step, _ = gathered(flat)
        conv_pieces = mine + [CORE(value) for value in mine]
        rest = after(packed(query_key_value_weight, pointwise_weight), step)
        rest_mine, _, late = gathered(rest)
        cotangent = after(attention_cotangent, late)
        index, relative = piece_order(), relative_order()
    else:
        all_flat = lax.all_gather(flat, "ctx", axis=1, tiled=True)
        all_point = lax.all_gather(pointwise_weight, "ctx", axis=0, tiled=True)
        all_projection = lax.all_gather(query_key_value_weight, "ctx", axis=0, tiled=True)
        conv_pieces = [all_flat[:, i * shard : (i + 1) * shard] for i in range(PIECES)]
        rest_pieces = [
            packed(
                all_projection[i * shard : (i + 1) * shard], all_point[i * slim : (i + 1) * slim]
            )
            for i in range(PIECES)
        ]
        index = relative = jnp.arange(PIECES, dtype=jnp.int32)
        cotangent = attention_cotangent

    even = lax.axis_index("ctx") % 2 == 0
    head, tail = tokens[:DILATION_STEP], tokens[rows - DILATION_STEP :]
    inner, outer = neighbours(
        jnp.where(even, tail, head), count, jnp.where(even, head, tail)
    )
    from_before, from_after = jnp.where(even, outer, inner), jnp.where(even, inner, outer)
    span = rows + 2 * DILATION_STEP
    start = lax.axis_index("ctx") * rows
    side = jnp.where(even, 1, -1)
    sides = jnp.stack([-side * rows, side * rows]).astype(jnp.int32)
    chain_pad = jnp.pad(chain_labels, (rows, rows), constant_values=-1)
    chain_rows = [
        lax.dynamic_slice_in_dim(chain_pad, start + (1 + offset) * rows, rows).reshape(1, rows)
        for offset in (side, 0, -side)
    ]
    chain_column = chain_rows[1].reshape(rows, 1)

    def bf16(*shape):
        return jax.ShapeDtypeStruct(shape, BF16)

    def f32(*shape):
        return jax.ShapeDtypeStruct(shape, F32)

    if quick:
        rest_pieces = rest_mine + [CORE(value) for value in rest_mine]
    results = (
        ((rows, narrow), F32),
        ((rows, narrow), BF16),
        ((rows, model), F32),
        ((model, columns), BF16),
        ((narrow, model), BF16),
    )
    query, kv, pre, hidden, mixed, projection, point = pl.pallas_call(
        front_kernel,
        out_shape=(bf16(rows, KEY_COLS), bf16(rows, columns - KEY_COLS))
        + tuple(pltpu.HBM(*result) for result in results),
        in_specs=[SMEM] + [VMEM] * 3 + [HBM] * (2 * PIECES),
        out_specs=(VMEM,) * 2 + (HBM,) * 5,
        scratch_shapes=[pltpu.VMEM(*result) for result in results]
        + [
            pltpu.VMEM((taps, model, narrow), BF16),
            pltpu.VMEM((span, model), BF16),
            pltpu.VMEM((PIECES, shard, narrow), BF16),
            pltpu.VMEM((narrow, model), F32),
            pltpu.SemaphoreType.DMA((3, PIECES)),
            pltpu.SemaphoreType.DMA((5,)),
        ],
        compiler_params=params(32),
        name="front",
    )(
        index,
        from_before,
        tokens,
        from_after,
        *[in_hbm(piece) for piece in conv_pieces + rest_pieces],
    )

    turning, kv = lax.optimization_barrier((tokens, kv))
    tokens_own, tokens_sent = pl.pallas_call(
        turn_kernel,
        out_shape=(pltpu.HBM((model // 2, span), BF16),) * 2,
        in_specs=[SMEM] + [VMEM] * 3,
        out_specs=(HBM,) * 2,
        scratch_shapes=[
            pltpu.VMEM((span, model), BF16),
            pltpu.VMEM((model, span), BF16),
            pltpu.VMEM((2, model // 2, span), BF16),
            pltpu.SemaphoreType.DMA((2,)),
        ],
        compiler_params=params(14),
        name="turn",
    )(relative, from_before, turning, from_after)

    d_prev, d_next = neighbours(cotangent, count)
    kv, d_prev, d_next = lax.optimization_barrier((kv, d_prev, d_next))
    kv_prev, kv_next = neighbours(kv, count)
    q_prev, q_next = neighbours(query, count)
    early = pl.pallas_call(
        attend_near_kernel,
        out_shape=(f32(2 * HEADS, rows, rows),) * 1,
        in_specs=[SMEM, SMEM, VMEM, HBM] + [VMEM] * 5,
        out_specs=(VMEM,) * 1,
        scratch_shapes=[pltpu.VMEM(kv.shape, BF16), pltpu.SemaphoreType.DMA(())],
        compiler_params=params(14),
        name="attend_near",
    )(
        slopes,
        sides,
        query,
        in_hbm(kv_prev),
        kv,
        attention_cotangent,
        chain_column,
        chain_rows[0],
        chain_rows[1],
    )
    kv_next, tokens_own, tokens_sent, early = lax.optimization_barrier(
        (kv_next, tokens_own, tokens_sent, early)
    )

    attended, d_query, stats = pl.pallas_call(
        attend_kernel,
        out_shape=(bf16(rows, HEADS * VAL), bf16(rows, KEY_COLS), f32(2 * HEADS, rows)),
        in_specs=[SMEM, SMEM, VMEM, HBM, VMEM, HBM] + [VMEM] * 6,
        out_specs=(VMEM,) * 3,
        scratch_shapes=[
            pltpu.VMEM(kv.shape, BF16),
            pltpu.VMEM(kv.shape, BF16),
            pltpu.SemaphoreType.DMA((2,)),
        ],
        compiler_params=params(20),
        name="attend",
    )(
        slopes,
        sides,
        query,
        in_hbm(kv_prev),
        kv,
        in_hbm(kv_next),
        attention_cotangent,
        chain_column,
        *chain_rows,
        *early,
    )

    s_prev, s_next = neighbours(stats, count)

    def key_grad(near, groups, more, kind, name):
        return pl.pallas_call(
            functools.partial(key_grad_kernel, near),
            out_shape=jax.ShapeDtypeStruct(kv.shape, kind),
            in_specs=[SMEM] * 2 + [VMEM] * (2 + 4 * len(groups) + len(more)),
            out_specs=VMEM,
            compiler_params=params(14),
            name=name,
        )(slopes, sides, kv, chain_column, *[ref for group in groups for ref in group], *more)

    own = key_grad(
        False, [(query, attention_cotangent, stats, chain_rows[1])], [], F32, "own_key_grad"
    )
    d_kv = key_grad(
        True,
        [(q_prev, d_prev, s_prev, chain_rows[0]), (q_next, d_next, s_next, chain_rows[2])],
        [own],
        BF16,
        "key_grad",
    )

    d_mixed, point_own, point_sent = pl.pallas_call(
        mix_back_kernel,
        out_shape=(bf16(rows, model),) + (f32(8, shard, narrow),) * 2,
        in_specs=[SMEM] + [VMEM] * 5,
        out_specs=(VMEM,) * 3,
        scratch_shapes=[pltpu.VMEM((narrow, model), F32)],
        compiler_params=params(20),
        name="mix_back",
    )(relative, d_query, d_kv, projection, mixed, hidden)

    own_shapes, sent_shapes = (
        (jax.ShapeDtypeStruct((4, 4 * shard, narrow), kind),) * 2
        for kind in (F32, BF16 if quick else F32)
    )
    shifted, *sent = pl.pallas_call(
        conv_back_kernel,
        out_shape=(bf16(span, wide),) + sent_shapes,
        in_specs=[VMEM] * 5,
        out_specs=(VMEM,) * 3,
        compiler_params=params(20),
        name="conv_back",
    )(d_mixed, point, pre, tokens_sent, point_sent)
    own = pl.pallas_call(
        conv_own_kernel,
        out_shape=own_shapes,
        in_specs=[VMEM] * 3,
        out_specs=(VMEM,) * 2,
        compiler_params=params(20),
        name="conv_own",
    )(shifted, tokens_own, point_own)

    if quick:
        total = scattered(own[1], own[0], sent[1], sent[0])
        dilated_grad, point_grad = unpack(total, model)
    else:
        parts = [
            unpack([block[i]], model) for block in (*own, *sent) for i in range(4)
        ]
        dilated_grad, point_grad = (
            lax.psum_scatter(
                jnp.concatenate([part[k] for part in parts], axis=0),
                "ctx",
                scatter_dimension=0,
                tiled=True,
            )
            for k in range(2)
        )
    return (attended, dilated_grad, point_grad)


def solution(mesh):
    return jax.shard_map(
        functools.partial(body, mesh.shape["ctx"]),
        mesh=mesh,
        in_specs=(
            P(("groups", "ctx"), None),
            P("ctx", None, None),
            P("ctx", None),
            P("ctx", None),
            P(),
            P("groups"),
            P(("groups", "ctx"), None),
        ),
        out_specs=(
            P(("groups", "ctx"), None),
            P(("groups", "ctx"), None, None),
            P(("groups", "ctx"), None),
        ),
        check_vma=False,
    )
```
